256 devices in a mesh: expert: 64 (over z, y, core), tensor: 4 (over x).
Axes of the slice: x: 4, y: 4, z: 8, core: 2. Of those that a mesh axis runs over, the one named last changes fastest.
Arguments:
- tokens: bfloat16 [8192, 2048], P('expert', 'tensor'), may hold values from -6 to 6
- grad_out: bfloat16 [8192, 2048], P('expert', 'tensor'), may hold values from -1.1953125 to 1.1953125
- routes: int32 [8192, 2], P('expert'), may hold values from 0 to 15, all different within a row; in each aligned block of 128 rows (0 to 127, 128 to 255, ...) at most 20 rows name the same one
- gates: float32 [8192, 2], P('expert'), may hold values from 0.1 to 1
- w_up: bfloat16 [2048, 131072], P(None, ('expert', 'tensor')), may hold values from -0.125 to 0.125
- w_down: bfloat16 [131072, 2048], P(('expert', 'tensor')), may hold values from -0.0625 to 0.0625
Outputs:
- grad_tokens: bfloat16 [8192, 2048], P('expert', 'tensor')
- grad_up: float32 [2048, 131072], P(None, ('expert', 'tensor'))
- grad_down: float32 [131072, 2048], P(('expert', 'tensor'))
The draws below stay inside these ranges and needn't reach their ends.
Inputs may be any that keep to these rules, and one draw needn't show every extreme that they name: `routes`: the two experts of a token differ. Among the tokens of one index of the expert axis no expert is named more than 20 times, and in every draw some expert is named exactly 20 times by the tokens of some index.
All inputs are finite; a program needn't handle non-finite values.
Results may differ from the reference program's by a relative error of at most 0.012.
Values may be sent and summed in bfloat16 or wider, within the bound.
A program may use at most 128 MiB of HBM per device.

```python
import math
import jax
import jax.numpy as jnp
import numpy as np
from jax import lax

D = 2048
HID = 8192
TOPK = 2
TOK_DEV = 128
EXPERTS = 16
GROUP = 4
CAP = 20
HID_DEV = 512
TOKENS = 8192
N_EXPERT = 64
N_TENSOR = 4


def level_of(stream_key, extent, shards, least, largest):
    def one(position, parts):
        steps = jax.random.uniform(jax.random.fold_in(jax.random.fold_in(stream_key, 6), position), (parts,), jnp.float32, least / len(shards), largest / len(shards))
        return jnp.repeat(jnp.exp(steps), extent[position] // parts).reshape((-1,) + (1,) * (len(extent) - position - 1))

    gain = one(*shards[0])
    for cut in shards[1:]:
        gain = gain * one(*cut)
    return gain


def assign_block(key, own, number, rows, count, top, reach, slope):
    sequence = jax.random.permutation(key, count)
    packed, common = load_shares(count, rows * top, reach, slope, True), load_shares(count, rows * top, reach, slope, False)
    places = jnp.arange(count)

    def named(lengths, offset_by):
        used = int((lengths > 0).sum())
        fixed = max(1, used // 4)
        shifted = fixed + (places - fixed + offset_by * (used - fixed)) % max(1, count - fixed)
        return jnp.zeros((count,), jnp.int32).at[sequence[jnp.where(places < fixed, places, shifted)]].set(jnp.asarray(lengths, jnp.int32))

    lengths = jnp.where(number % 4 == 0, named(packed, number // 4), named(common, number - number // 4 - 1))
    mixed = jax.random.permutation(jax.random.fold_in(own, 3), count)
    giver, receiver = mixed[0:count // 2 * 2:2], mixed[1:count // 2 * 2:2]
    slack = jnp.minimum(lengths[giver] - 1, reach - lengths[receiver]) // 2
    slack = jnp.where((giver == sequence[0]) | (receiver == sequence[0]) | (lengths[receiver] == 0), 0, jnp.maximum(slack, 0))
    shifted = jax.random.randint(jax.random.fold_in(own, 4), (count // 2,), 0, 1 << 20) % (slack + 1)
    lengths = lengths.at[giver].add(-shifted).at[receiver].add(shifted)
    items = jnp.searchsorted(jnp.cumsum(lengths), jnp.arange(rows * top), side="right").astype(jnp.int32)
    grid = items.reshape(top, rows).T
    grid = grid[jax.random.permutation(jax.random.fold_in(own, 1), rows)]
    offset_by = jax.random.randint(jax.random.fold_in(own, 2), (rows, 1), 0, top)
    return jnp.take_along_axis(grid, (jnp.arange(top)[None, :] + offset_by) % top, axis=1)


def load_shares(count, total, reach, lean, full):
    portions = [(1 << 20) // math.isqrt(standing ** lean) + 1 for standing in range(1, count + 1)]
    largest = reach if full else min(reach, max(-(-total // count), total * portions[0] // sum(portions)))
    least = 1 if total - largest >= count - 1 else 0
    given, rest = [largest] + [least] * (count - 1), total - largest - least * (count - 1)
    while rest > 0:
        free = [i for i in range(1, count) if given[i] < largest] or [i for i in range(1, count) if given[i] < reach]
        pool, left = sum([portions[i] for i in free]), rest
        for i in free:
            extra = min(reach - given[i], max(1, left * portions[i] // pool), rest)
            given[i] = given[i] + extra
            rest = rest - extra
    return np.array(given)


def scatter_about(own_key, dims, deviation, most, pieces=(), kind=jnp.bfloat16):
    result = deviation * jax.random.normal(own_key, dims, jnp.float32)
    if pieces:
        result = result * level_of(own_key, dims, pieces, -0.22, 0.18)
    return jnp.clip(result, -most, most).astype(kind)


def setup_inputs(seed: int = 0) -> dict:
    arg_keys = jax.random.split(jax.random.key(seed), 7)
    tokens = scatter_about(arg_keys[0], (TOKENS, D), 1.0, 6.0, ((0, 64), (1, 4)))
    grad_out = scatter_about(arg_keys[1], (TOKENS, D), 0.2, 1.1953125, ((0, 64), (1, 4)))
    routes_keys = jax.random.split(jax.random.fold_in(arg_keys[2], 1), TOKENS // TOK_DEV)
    routes_turns = jax.random.permutation(jax.random.fold_in(arg_keys[2], 3), TOKENS // TOK_DEV)
    routes = jax.vmap(lambda own, number: assign_block(jax.random.fold_in(arg_keys[2], 2), own, number, TOK_DEV, EXPERTS, TOPK, CAP, 2))(routes_keys, routes_turns).reshape((TOKENS, TOPK))
    gates = jnp.clip(jnp.exp(math.log(1.0) - 2.3025851 * jax.random.uniform(arg_keys[3], (TOKENS, TOPK), jnp.float32) ** level_of(arg_keys[3], (TOKENS, TOPK), ((0, 64),), -0.2, 0.2)), 0.1, 1.0)
    w_up = scatter_about(arg_keys[4], (D, EXPERTS * HID), D ** -0.5, 0.125, ((1, 256),))
    w_down = scatter_about(arg_keys[5], (EXPERTS * HID, D), HID ** -0.5, 0.0625, ((0, 256),))
    return dict(tokens=tokens, grad_out=grad_out, routes=routes, gates=gates, w_up=w_up, w_down=w_down)


root_half = 0.7071067811865476
gauss_norm = 0.3989422804014327


def gelu_value(v):
    return 0.5 * v * (1.0 + lax.erf(v * root_half))


def gelu_slope(v):
    return 0.5 * (1.0 + lax.erf(v * root_half)) + v * jnp.exp(-0.5 * v * v) * gauss_norm


def slot_targets(routes):
    flat = routes.reshape(N_EXPERT, TOK_DEV * TOPK).astype(jnp.int32)
    onehot = (flat[:, :, None] == jnp.arange(EXPERTS, dtype=jnp.int32)[None, None, :]).astype(jnp.int32)
    rank = (jnp.cumsum(onehot, axis=1, dtype=jnp.int32) - onehot).astype(jnp.int32)
    slot = jnp.sum(rank * onehot, axis=2).astype(jnp.int32)
    return (flat * CAP + slot).astype(jnp.int32)


def slice_sum(d_pre, up_e):
    count = GROUP * N_TENSOR

    def step(total, index):
        left = lax.dynamic_slice_in_dim(d_pre, index * HID_DEV, HID_DEV, 1)
        right = lax.dynamic_slice_in_dim(up_e, index * HID_DEV, HID_DEV, 1)
        term = jnp.dot(left, right.T, preferred_element_type=jnp.float32)
        return total + lax.optimization_barrier(term.astype(jnp.bfloat16)).astype(jnp.float32), None

    start = jnp.zeros((d_pre.shape[0], up_e.shape[0]), jnp.float32)
    total, unused = lax.scan(step, start, jnp.arange(count, dtype=jnp.int32))
    return total


def per_expert(operands):
    rows_x, rows_y, up_e, down_e = operands
    pre = jnp.dot(rows_x, up_e, preferred_element_type=jnp.float32)
    act = gelu_value(pre).astype(jnp.bfloat16)
    d_act = jnp.dot(rows_y, down_e.T, preferred_element_type=jnp.float32)
    d_pre = (d_act * gelu_slope(pre)).astype(jnp.bfloat16)
    grad_up_e = jnp.dot(rows_x.T, d_pre, preferred_element_type=jnp.float32)
    grad_down_e = jnp.dot(act.T, rows_y, preferred_element_type=jnp.float32)
    return grad_up_e, grad_down_e, slice_sum(d_pre, up_e)


def reference(tokens, grad_out, routes, gates, w_up, w_down):
    dest = slot_targets(routes)
    repeated = jnp.repeat(tokens.reshape(N_EXPERT, TOK_DEV, D), TOPK, axis=1)
    scaled = (grad_out[:, None, :].astype(jnp.float32) * gates[:, :, None]).astype(jnp.bfloat16)
    scaled = scaled.reshape(N_EXPERT, TOK_DEV * TOPK, D)
    source = jnp.arange(N_EXPERT, dtype=jnp.int32)[:, None]

    def place(values):
        buffer = jnp.zeros((N_EXPERT, EXPERTS * CAP, D), jnp.bfloat16)
        buffer = buffer.at[source, dest].set(values)
        buffer = buffer.reshape(N_EXPERT, EXPERTS, CAP, D).transpose(1, 0, 2, 3)
        return buffer.reshape(EXPERTS, N_EXPERT * CAP, D)

    slots_x = place(repeated)
    slots_y = place(scaled)
    ups = w_up.reshape(D, EXPERTS, HID).transpose(1, 0, 2)
    downs = w_down.reshape(EXPERTS, HID, D)
    grads_up, grads_down, slot_grads = lax.map(per_expert, (slots_x, slots_y, ups, downs))
    grad_up = grads_up.transpose(1, 0, 2).reshape(D, EXPERTS * HID)
    grad_down = grads_down.reshape(EXPERTS * HID, D)
    slot_grads = slot_grads.reshape(EXPERTS, N_EXPERT, CAP, D).transpose(1, 0, 2, 3).reshape(N_EXPERT, EXPERTS * CAP, D)
    picked = jnp.take_along_axis(slot_grads, dest[:, :, None], axis=1)
    grad_tokens = picked.reshape(N_EXPERT, TOK_DEV, TOPK, D).sum(axis=2).reshape(TOKENS, D).astype(jnp.bfloat16)
    return (grad_tokens, grad_up, grad_down)
```

```python
import jax
import jax.numpy as jnp
from jax import lax
from jax.experimental import pallas as pl
from jax.experimental.pallas import tpu as pltpu
from jax.sharding import PartitionSpec as P

MESH = pl.DeviceIdType.MESH
Z, Y, X = 8, 4, 4
CAP, PAIR = 20, 40
EXPERTS = 16
BLOCKS = 32
TOK = 128
QUARTER = 512
HALF = 256
D = 2048
NEAR = (0, 1, 7, 2, 6, 3, 5, 4)

root_half = 0.7071067811865476
gauss_norm = 0.3989422804014327


def gelu_value(v):
    return 0.5 * v * (1.0 + lax.erf(v * root_half))


def gelu_slope(v):
    return 0.5 * (1.0 + lax.erf(v * root_half)) + v * jnp.exp(-0.5 * v * v) * gauss_norm


def place():
    e = lax.axis_index("expert")
    x = lax.axis_index("tensor")
    return e // 8, (e // 2) % 4, e % 2, x


def device(z, y, c, x):
    return ((z * Y + y) * 2 + c, x)


class Net:
    def __init__(self, send_sem, recv_sem):
        self.send_sem, self.recv_sem, self.count, self.sent = send_sem, recv_sem, 0, []

    def number(self):
        self.count += 1
        return self.count - 1

    def send(self, src, dst, target, start=True):
        i = self.number()
        copy = pltpu.make_async_remote_copy(
            src_ref=src,
            dst_ref=dst,
            send_sem=self.send_sem.at[i],
            recv_sem=self.recv_sem.at[i],
            device_id=target,
            device_id_type=MESH,
        )
        if start:
            copy.start()
        self.sent.append(copy)
        return copy

    def finish(self):
        for copy in self.sent:
            copy.wait_send()


def meet(z, y, c, x):
    barrier = pltpu.get_barrier_semaphore()
    partner = y + 1 - 2 * (y % 2)
    others = [
        device(z, y, 1 - c, x),
        device(z, partner, c, x),
        device(z, y, c, (x + 1) % X),
        device(z, y, c, (x + 3) % X),
    ]
    for dz in range(Z):
        for j in range(2):
            if dz or j:
                others.append(device((z + dz) % Z, y if j == 0 else 3 - y, c, x))
    for other in others:
        pl.semaphore_signal(barrier, inc=1, device_id=other, device_id_type=MESH)
    pl.semaphore_wait(barrier, len(others))


def gather_kernel(
    routes, gates, tok, grad, xy, sel, route_buf, gate_buf, values, slots, send_sem, recv_sem, own_sem
):
    z, y, c, x = place()
    k = ((y + 1) // 2) % 2
    partner = y + 1 - 2 * (y % 2)
    net = Net(send_sem, recv_sem)
    meet(z, y, c, x)

    mate = device(z, y, 1 - c, x)
    first = net.send(routes, route_buf.at[c], mate)
    second = net.send(gates, gate_buf.at[c], mate)
    i = net.number()

    def value_copy(src):
        return pltpu.make_async_remote_copy(
            src_ref=src,
            dst_ref=values.at[c],
            send_sem=send_sem.at[i],
            recv_sem=recv_sem.at[i],
            device_id=mate,
            device_id_type=MESH,
        )

    @pl.when(c == 0)
    def _():
        value_copy(grad).start()

    @pl.when(c == 1)
    def _():
        value_copy(tok).start()

    third = value_copy(tok)
    net.sent.append(third)
    route_buf[c] = routes[...]
    gate_buf[c] = gates[...]
    values[c] = jnp.where(c == 0, tok[...], grad[...])
    first.wait_recv()
    second.wait_recv()
    third.wait_recv()

    row = lax.broadcasted_iota(jnp.int32, (EXPERTS * PAIR, TOK), 0)
    expert = lax.broadcasted_iota(jnp.int32, (EXPERTS, TOK), 0)
    before = (
        lax.broadcasted_iota(jnp.int32, (TOK, TOK), 0)
        < lax.broadcasted_iota(jnp.int32, (TOK, TOK), 1)
    ).astype(jnp.bfloat16)
    scale = jnp.zeros((EXPERTS * PAIR, 1), jnp.float32)
    total = jnp.zeros((EXPERTS * PAIR, QUARTER), jnp.float32)
    for s in range(2):
        r = route_buf[s]
        g = gate_buf[s]
        named0 = (expert == r[0:1]).astype(jnp.float32)
        named1 = (expert == r[1:2]).astype(jnp.float32)
        earlier = jnp.dot(
            (named0 + named1).astype(jnp.bfloat16), before, preferred_element_type=jnp.float32
        )
        slot0 = jnp.sum(named0 * earlier, axis=0, keepdims=True).astype(jnp.int32)
        slot1 = jnp.sum(named1 * earlier, axis=0, keepdims=True).astype(jnp.int32)
        hit0 = row == r[0:1] * PAIR + s * CAP + slot0
        hit1 = row == r[1:2] * PAIR + s * CAP + slot1
        pick = jnp.where(hit0 | hit1, 1.0, 0.0).astype(jnp.bfloat16)
        weight = jnp.where(hit0, g[0:1], 0.0) + jnp.where(hit1, g[1:2], 0.0)
        scale = scale + jnp.sum(weight, axis=1, keepdims=True)
        sel[:, s * TOK : (s + 1) * TOK] = pick
        total = total + jnp.dot(pick, values[s], preferred_element_type=jnp.float32)
    total = total * jnp.where(c == 0, 1.0, scale)
    slots[...] = total.astype(jnp.bfloat16).reshape(EXPERTS, PAIR, QUARTER)

    def cols(q):
        return pl.ds(pl.multiple_of(q * QUARTER, QUARTER), QUARTER)

    arrivals = {}
    mine = z * 4 + k * 2 + y // 2
    own_copy = None
    for dz in NEAR:
        ze = (z + dz) % Z
        for j in range(2):
            expert_id = ze * 2 + (y // 2 if j == 0 else 1 - y // 2)
            src = slots.at[expert_id]
            dst = xy.at[c, mine, :, cols(x)]
            if dz == 0 and j == 0:
                own_copy = pltpu.make_async_copy(src, dst, own_sem)
                own_copy.start()
            else:
                arrivals[dz, j] = net.send(src, dst, device(ze, y if j == 0 else 3 - y, c, x))

    right, left = (x + 1) % X, (x + 3) % X
    far = (x + 2) % X
    to_right, to_left = device(z, y, c, right), device(z, y, c, left)
    to_y = device(z, partner, c, x)
    live = [dict() for _ in NEAR]

    def part(block, count, q):
        return xy.at[c, pl.ds(block, count), :, cols(q)]

    def both(block, count, q, target):
        return net.send(part(block, count, q), part(block, count, q), target)

    def step_a(n):
        dz, at = NEAR[n], live[n]
        if dz == 0:
            own_copy.wait()
        else:
            arrivals[dz, 0].wait_recv()
        arrivals[dz, 1].wait_recv()
        base = ((z + Z - dz) % Z) * 4
        at["base"], at["own"], at["other"] = base, base + k * 2, base + (1 - k) * 2
        at["r"] = both(at["own"], 2, x, to_right)
        at["l"] = both(at["own"], 2, x, to_left)
        at["y"] = both(at["own"], 2, x, to_y)

    def step_b(n):
        at = live[n]
        at["r"].wait_recv()
        at["l"].wait_recv()
        if n % 2 == 0:
            at["y"].wait_recv()
            at["r2"] = both(at["other"], 2, x, to_right)
            at["l2"] = both(at["other"], 2, x, to_left)
        else:
            at["fr"] = both(at["own"], 1, left, to_right)
            at["fl"] = both(at["own"] + 1, 1, right, to_left)
            at["y1"] = both(at["own"], 2, left, to_y)
            at["y2"] = both(at["own"], 2, right, to_y)

    def step_c(n):
        at = live[n]
        if n % 2 == 0:
            at["r2"].wait_recv()
            at["l2"].wait_recv()
            at["fr"] = both(at["base"], 2, left, to_right)
            at["fl"] = both(at["base"] + 2, 2, right, to_left)
        else:
            at["fr"].wait_recv()
            at["fl"].wait_recv()
            at["y3"] = both(at["own"], 2, far, to_y)

    def step_d(n):
        at = live[n]
        if n % 2 == 0:
            at["fr"].wait_recv()
            at["fl"].wait_recv()
        else:
            for name in ("y", "y1", "y2", "y3"):
                at[name].wait_recv()
        rows = xy.at[c, pl.ds(at["base"], 4)]
        at["mate"] = net.send(rows, rows, mate)

    for i in range(len(NEAR) + 3):
        for lag, step in ((3, step_d), (2, step_c), (1, step_b), (0, step_a)):
            if 0 <= i - lag < len(NEAR):
                step(i - lag)
    for at in live:
        at["mate"].wait_recv()
    net.finish()


def return_kernel(
    partial, sel, out, acc, from_mate, hop_a, hop_b, from_y, slots, result, final, send_sem, recv_sem, own_sem
):
    z, y, c, x = place()
    k = ((y + 1) // 2) % 2
    partner = y + 1 - 2 * (y % 2)
    net = Net(send_sem, recv_sem)
    meet(z, y, c, x)
    mate = device(z, y, 1 - c, x)
    right, left = (x + 1) % X, (x + 3) % X
    far = (x + 2) % X
    to_right, to_left = device(z, y, c, right), device(z, y, c, left)
    to_y = device(z, partner, c, x)
    order = NEAR[::-1]
    live = [dict() for _ in order]

    def cols(q, core):
        return pl.ds(pl.multiple_of(q * QUARTER + core * HALF, HALF), HALF)

    def add(ref, other):
        ref[...] = (ref[...].astype(jnp.float32) + other[...].astype(jnp.float32)).astype(jnp.bfloat16)

    for n, dz in enumerate(order):
        base = ((z + dz) % Z) * 4
        live[n]["base"] = base
        live[n]["mate"] = [
            net.send(
                partial.at[pl.ds(base, 4), :, cols(q, 1 - c)], from_mate.at[q, pl.ds(base, 4)], mate
            )
            for q in range(4)
        ]

    def step_a(n):
        at = live[n]
        base = at["base"]
        for q in range(4):
            at["mate"][q].wait_recv()
            acc[q, pl.ds(base, 4)] = (
                partial[pl.ds(base, 4), :, cols(q, c)].astype(jnp.float32)
                + from_mate[q, pl.ds(base, 4)].astype(jnp.float32)
            ).astype(jnp.bfloat16)
        at["ar"] = net.send(acc.at[far, pl.ds(base, 2)], hop_a.at[n, 0], to_right)
        at["al"] = net.send(acc.at[far, pl.ds(base + 2, 2)], hop_a.at[n, 1], to_left)

    def step_b(n):
        at = live[n]
        base = at["base"]
        at["ar"].wait_recv()
        add(acc.at[right, pl.ds(base, 2)], hop_a.at[n, 0])
        at["al"].wait_recv()
        add(acc.at[left, pl.ds(base + 2, 2)], hop_a.at[n, 1])
        at["br"] = net.send(acc.at[right, pl.ds(base, 4)], hop_b.at[n, 0], to_right)
        at["bl"] = net.send(acc.at[left, pl.ds(base, 4)], hop_b.at[n, 1], to_left)

    def step_c(n):
        at = live[n]
        base = at["base"]
        at["br"].wait_recv()
        at["bl"].wait_recv()
        ref = acc.at[x, pl.ds(base, 4)]
        ref[...] = (
            ref[...].astype(jnp.float32)
            + hop_b[n, 0].astype(jnp.float32)
            + hop_b[n, 1].astype(jnp.float32)
        ).astype(jnp.bfloat16)
        at["y"] = net.send(acc.at[x, pl.ds(base + (1 - k) * 2, 2)], from_y.at[n], to_y)

    me = z * 2 + y // 2

    def step_d(n):
        at, dz = live[n], order[n]
        base = at["base"] + k * 2
        at["y"].wait_recv()
        add(acc.at[x, pl.ds(base, 2)], from_y.at[n])
        zs = (z + dz) % Z
        at["back"] = []
        for j in range(2):
            src = acc.at[x, base + (y // 2 if j == 0 else 1 - y // 2)]
            dst = slots.at[me]
            if dz == 0 and j == 0:
                copy = pltpu.make_async_copy(src, dst, own_sem)
                copy.start()
                at["local"] = copy
            else:
                at["back"].append(net.send(src, dst, device(zs, y if j == 0 else 3 - y, c, x)))

    for i in range(len(order) + 3):
        for lag, step in ((3, step_d), (2, step_c), (1, step_b), (0, step_a)):
            if 0 <= i - lag < len(order):
                step(i - lag)
    for at in live:
        for copy in at["back"]:
            copy.wait_recv()
        if "local" in at:
            at["local"].wait()
    combined = lax.dot_general(
        sel[...],
        slots[...].reshape(EXPERTS * PAIR, HALF),
        (((0,), (0,)), ((), ())),
        preferred_element_type=jnp.float32,
    )
    result[...] = combined.astype(jnp.bfloat16).reshape(2, TOK, HALF)
    last = net.send(result.at[1 - c], final, mate)
    last.wait_recv()

    @pl.when(c == 0)
    def _():
        out[:, 0:HALF] = result[0]
        out[:, HALF:QUARTER] = final[...]

    @pl.when(c == 1)
    def _():
        out[:, 0:HALF] = final[...]
        out[:, HALF:QUARTER] = result[1]

    net.finish()


def vmem():
    return pl.BlockSpec(memory_space=pltpu.VMEM)


def anywhere():
    return pl.BlockSpec(memory_space=pl.ANY)


def local(tokens, grad_out, routes, gates, w_up, w_down):
    bf16 = jnp.bfloat16
    xy, sel = pl.pallas_call(
        gather_kernel,
        out_shape=(
            jax.ShapeDtypeStruct((2, BLOCKS, PAIR, D), bf16),
            jax.ShapeDtypeStruct((EXPERTS * PAIR, 2 * TOK), bf16),
        ),
        in_specs=[vmem()] * 4,
        out_specs=(anywhere(), vmem()),
        scratch_shapes=[
            pltpu.VMEM((2, 2, TOK), jnp.int32),
            pltpu.VMEM((2, 2, TOK), jnp.float32),
            pltpu.VMEM((2, TOK, QUARTER), bf16),
            pltpu.VMEM((EXPERTS, PAIR, QUARTER), bf16),
            pltpu.SemaphoreType.DMA((110,)),
            pltpu.SemaphoreType.DMA((110,)),
            pltpu.SemaphoreType.DMA,
        ],
        compiler_params=pltpu.CompilerParams(collective_id=0, has_side_effects=True),
        name="gather_slots",
    )(routes.T, gates.T, tokens, grad_out)
    rows = xy.reshape(2, BLOCKS * PAIR, D)
    rows_x, rows_y = rows[0], rows[1]
    pre = jnp.dot(rows_x, w_up, preferred_element_type=jnp.float32)
    act = gelu_value(pre).astype(bf16)
    d_act = lax.dot_general(
        rows_y, w_down, (((1,), (1,)), ((), ())), preferred_element_type=jnp.float32
    )
    d_pre = (d_act * gelu_slope(pre)).astype(bf16)
    partial = lax.dot_general(
        d_pre, w_up, (((1,), (1,)), ((), ())), preferred_element_type=jnp.float32
    ).astype(bf16)
    grad_tokens = pl.pallas_call(
        return_kernel,
        out_shape=jax.ShapeDtypeStruct((TOK, QUARTER), bf16),
        in_specs=[vmem()] * 2,
        out_specs=vmem(),
        scratch_shapes=[
            pltpu.VMEM((4, BLOCKS, PAIR, HALF), bf16),
            pltpu.VMEM((4, BLOCKS, PAIR, HALF), bf16),
            pltpu.VMEM((Z, 2, 2, PAIR, HALF), bf16),
            pltpu.VMEM((Z, 2, 4, PAIR, HALF), bf16),
            pltpu.VMEM((Z, 2, PAIR, HALF), bf16),
            pltpu.VMEM((EXPERTS, PAIR, HALF), bf16),
            pltpu.VMEM((2, TOK, HALF), bf16),
            pltpu.VMEM((TOK, HALF), bf16),
            pltpu.SemaphoreType.DMA((100,)),
            pltpu.SemaphoreType.DMA((100,)),
            pltpu.SemaphoreType.DMA,
        ],
        compiler_params=pltpu.CompilerParams(
            collective_id=1, has_side_effects=True, vmem_limit_bytes=40 * 1024 * 1024
        ),
        name="return_slots",
    )(partial.reshape(BLOCKS, PAIR, D), sel)
    grad_up = lax.dot_general(
        rows_x, d_pre, (((0,), (0,)), ((), ())), preferred_element_type=jnp.float32
    )
    grad_down = lax.dot_general(
        act, rows_y, (((0,), (0,)), ((), ())), preferred_element_type=jnp.float32
    )
    return (grad_tokens, grad_up, grad_down)


def solution(mesh):
    return jax.shard_map(
        local,
        mesh=mesh,
        in_specs=(
            P("expert", "tensor"),
            P("expert", "tensor"),
            P("expert", None),
            P("expert", None),
            P(None, ("expert", "tensor")),
            P(("expert", "tensor"), None),
        ),
        out_specs=(
            P("expert", "tensor"),
            P(None, ("expert", "tensor")),
            P(("expert", "tensor"), None),
        ),
        check_vma=False,
    )
```

```python
import jax
import jax.numpy as jnp
from jax import lax
from jax.experimental import pallas as pl
from jax.experimental.pallas import tpu as pltpu
from jax.sharding import PartitionSpec as P

MESH = pl.DeviceIdType.MESH
Z, Y, X = 8, 4, 4
CAP, PAIR = 20, 40
EXPERTS = 16
BLOCKS = 32
ROWS = BLOCKS * PAIR
TOK = 128
QUARTER = 512
HALF = 256
D = 2048
HID_DEV = 512
TILE = 256
NEAR = (0, 1, 7, 2, 6, 3, 5, 4)
MODES = (0, 0, 1, 1, 1, 0, 0, 1)
RETURN_MODES = (0, 0, 0, 0, 0, 1, 1, 0)
GROUPS = ((0, 1), (2, 3), (4, 5), (6, 7))
ORDER = (
    "A0", "A1", "A2", "B0", "B1", "A3", "A4", "Br2", "Bl2", "Cr0", "Cl0", "A5", "A6", "Cr1", "Cl1",
    "Br3", "Bl3", "A7", "Br4", "Bl4", "C2", "B5", "D0", "B6", "D1", "C3", "F0", "C4", "Br7", "Bl7",
    "Cr5", "Cl5", "D2", "RA0", "Cr6", "Cl6", "RA1", "C7", "D3", "D5", "D4", "RB0", "F1", "RX0",
    "RB1", "RX1", "D6", "F2", "RA3", "RA2", "RC0", "D7", "RA4", "RC1", "RA5", "RB3", "RX3", "RD0",
    "RB2", "RX2", "F3", "RB4", "RX4", "RC3", "RD1", "GU0", "GD0", "RA6", "RY5", "RC2", "RA7", "GU1",
    "RD3", "GD1", "RC4", "GU2", "RB5", "RX5", "GD2", "RB7", "RX7", "GU3", "GD3", "GU4", "RY6",
    "RC5", "RD2", "GD4", "GU5", "RC7", "RD4", "GD5", "RB6", "RX6", "GU6", "GD6", "GU7", "RD7",
    "GD7", "RC6",
)

root_half = 0.7071067811865476
gauss_norm = 0.3989422804014327


def gelu_value(v):
    return 0.5 * v * (1.0 + lax.erf(v * root_half))


def gelu_slope(v):
    return 0.5 * (1.0 + lax.erf(v * root_half)) + v * jnp.exp(-0.5 * v * v) * gauss_norm


def place():
    e = lax.axis_index("expert")
    x = lax.axis_index("tensor")
    return e // 8, (e // 2) % 4, e % 2, x


def device(z, y, c, x):
    return ((z * Y + y) * 2 + c, x)


class Net:
    def __init__(self, send_sem, recv_sem):
        self.send_sem, self.recv_sem, self.count, self.sent = send_sem, recv_sem, 0, []

    def make(self, src, dst, target):
        i = self.count
        self.count += 1
        copy = pltpu.make_async_remote_copy(
            src_ref=src,
            dst_ref=dst,
            send_sem=self.send_sem.at[i],
            recv_sem=self.recv_sem.at[i],
            device_id=target,
            device_id_type=MESH,
        )
        self.sent.append(copy)
        return copy

    def send(self, src, dst, target):
        copy = self.make(src, dst, target)
        copy.start()
        return copy

    def finish(self):
        for copy in self.sent:
            copy.wait_send()


def kernel(
    routes, gates, tok, grad, w_up, w_down,
    out, grad_up, grad_down,
    route_buf, gate_buf, values, sel, send_slots, xy, wu, wd, act, d_pre, part, from_mate, acc,
    hop_a, hop_b, from_y, slots, result, final, tile_up, tile_down,
    send_sem, recv_sem, own_sem, tile_sem,
):
    z, y, c, x = place()
    k = ((y + 1) // 2) % 2
    partner = y + 1 - 2 * (y % 2)
    net = Net(send_sem, recv_sem)
    mate = device(z, y, 1 - c, x)
    right, left, far = (x + 1) % X, (x + 3) % X, (x + 2) % X
    to_right, to_left = device(z, y, c, right), device(z, y, c, left)
    to_y = device(z, partner, c, x)

    others = [mate, to_y, to_right, to_left]
    for dz in range(Z):
        for j in range(2):
            if dz or j:
                others.append(device((z + dz) % Z, y if j == 0 else 3 - y, c, x))
    barrier = pltpu.get_barrier_semaphore()
    for other in others:
        pl.semaphore_signal(barrier, inc=1, device_id=other, device_id_type=MESH)

    up_copy = pltpu.make_async_copy(w_up, wu, own_sem.at[0])
    down_copy = pltpu.make_async_copy(w_down, wd, own_sem.at[1])
    up_copy.start()
    down_copy.start()

    row = lax.broadcasted_iota(jnp.int32, (EXPERTS * PAIR, TOK), 0)
    expert = lax.broadcasted_iota(jnp.int32, (EXPERTS, TOK), 0)
    before = (
        lax.broadcasted_iota(jnp.int32, (TOK, TOK), 0)
        < lax.broadcasted_iota(jnp.int32, (TOK, TOK), 1)
    ).astype(jnp.bfloat16)

    def choose(r, g, s):
        named0 = (expert == r[0:1]).astype(jnp.float32)
        named1 = (expert == r[1:2]).astype(jnp.float32)
        earlier = jnp.dot(
            (named0 + named1).astype(jnp.bfloat16), before, preferred_element_type=jnp.float32
        )
        slot0 = jnp.sum(named0 * earlier, axis=0, keepdims=True).astype(jnp.int32)
        slot1 = jnp.sum(named1 * earlier, axis=0, keepdims=True).astype(jnp.int32)
        hit0 = row == r[0:1] * PAIR + s * CAP + slot0
        hit1 = row == r[1:2] * PAIR + s * CAP + slot1
        pick = jnp.where(hit0 | hit1, 1.0, 0.0).astype(jnp.bfloat16)
        weight = jnp.where(hit0, g[0:1], 0.0) + jnp.where(hit1, g[1:2], 0.0)
        return pick, jnp.sum(weight, axis=1, keepdims=True)

    mine = jnp.where(c == 0, tok[...], grad[...])
    pick, scale = choose(routes[...], gates[...], c)
    sel[c] = pick
    total = jnp.dot(pick, mine, preferred_element_type=jnp.float32)

    pl.semaphore_wait(barrier, len(others))
    first = net.send(routes, route_buf, mate)
    second = net.send(gates, gate_buf, mate)
    third = net.make(tok, values, mate)

    @pl.when(c == 0)
    def _():
        pltpu.make_async_remote_copy(
            src_ref=grad, dst_ref=values, send_sem=send_sem.at[2], recv_sem=recv_sem.at[2],
            device_id=mate, device_id_type=MESH,
        ).start()

    @pl.when(c == 1)
    def _():
        third.start()

    first.wait_recv()
    second.wait_recv()
    pick, more = choose(route_buf[...], gate_buf[...], 1 - c)
    sel[1 - c] = pick
    scale = scale + more
    third.wait_recv()
    total = total + jnp.dot(pick, values[...], preferred_element_type=jnp.float32)
    total = total * jnp.where(c == 0, 1.0, scale)
    send_slots[...] = total.astype(jnp.bfloat16).reshape(EXPERTS, PAIR, QUARTER)

    def cols(q, core=None):
        if core is None:
            return pl.ds(pl.multiple_of(q * QUARTER, QUARTER), QUARTER)
        return pl.ds(pl.multiple_of(q * QUARTER + core * HALF, HALF), HALF)

    ev = {}
    for n, dz in enumerate(NEAR):
        ze = (z + dz) % Z
        for j in range(2):
            src = send_slots.at[ze * 2 + (y // 2 if j == 0 else 1 - y // 2)]
            dst = xy.at[c, n * 4 + k * 2 + y // 2, :, cols(x)]
            if dz == 0 and j == 0:
                local_slots = pltpu.make_async_copy(src, dst, own_sem.at[2])
                local_slots.start()
            else:
                ev["z", n, j] = net.send(src, dst, device(ze, y if j == 0 else 3 - y, c, x))

    def share(key, block, count, q, target):
        ref = xy.at[c, pl.ds(block, count), :, cols(q)]
        ev[key] = net.send(ref, ref, target)

    def got(*keys):
        for key in keys:
            if key not in done:
                done.add(key)
                ev[key].wait_recv()

    done = set()

    def step_A(n):
        if n == 0:
            local_slots.wait()
        else:
            got(("z", n, 0))
        got(("z", n, 1))
        own = n * 4 + k * 2
        share(("r", n), own, 2, x, to_right)
        share(("l", n), own, 2, x, to_left)
        share(("y", n), own, 2, x, to_y)

    def step_B(n):
        got(("y", n))
        other = n * 4 + (1 - k) * 2
        share(("r2", n), other, 2, x, to_right)
        share(("l2", n), other, 2, x, to_left)

    def step_Cr(n):
        got(("r", n), ("r2", n))
        share(("fr", n), n * 4, 2, left, to_right)

    def step_Cl(n):
        got(("l", n), ("l2", n))
        share(("fl", n), n * 4 + 2, 2, right, to_left)

    def step_Br(n):
        got(("r", n))
        own = n * 4 + k * 2
        share(("fr", n), own, 1, left, to_right)
        share(("y1", n), own, 2, left, to_y)

    def step_Bl(n):
        got(("l", n))
        own = n * 4 + k * 2
        share(("fl", n), own + 1, 1, right, to_left)
        share(("y2", n), own, 2, right, to_y)

    def step_C(n):
        got(("fr", n), ("fl", n))
        share(("y3", n), n * 4 + k * 2, 2, far, to_y)

    def step_D(n):
        if MODES[n]:
            got(("y", n), ("y1", n), ("y2", n), ("y3", n))
        else:
            got(("fr", n), ("fl", n))
        ref = xy.at[c, pl.ds(n * 4, 4)]
        ev["m", n] = net.send(ref, ref, mate)

    def step_F(g):
        if g == 0:
            up_copy.wait()
            down_copy.wait()
        got(*[("m", n) for n in GROUPS[g]])
        first_block, count = GROUPS[g][0] * 4, len(GROUPS[g]) * 4
        rows, size = pl.ds(first_block * PAIR, count * PAIR), count * PAIR
        rows_x = xy[0, pl.ds(first_block, count)].reshape(size, D)
        rows_y = xy[1, pl.ds(first_block, count)].reshape(size, D)
        pre = jnp.dot(rows_x, wu[...], preferred_element_type=jnp.float32)
        d_act = lax.dot_general(
            rows_y, wd[...], (((1,), (1,)), ((), ())), preferred_element_type=jnp.float32
        )
        act[rows] = gelu_value(pre).astype(jnp.bfloat16)
        slope = (d_act * gelu_slope(pre)).astype(jnp.bfloat16)
        d_pre[rows] = slope
        product = lax.dot_general(
            slope, wu[...], (((1,), (1,)), ((), ())), preferred_element_type=jnp.float32
        )
        part[pl.ds(first_block, count)] = product.astype(jnp.bfloat16).reshape(count, PAIR, D)
        for n in GROUPS[g]:
            for q in range(4):
                ev["p", n, q] = net.send(
                    part.at[pl.ds(n * 4, 4), :, cols(q, 1 - c)], from_mate.at[q, pl.ds(n * 4, 4)], mate
                )

    def wide(value):
        return value.astype(jnp.float32)

    def add(ref, other):
        ref[...] = (wide(ref[...]) + wide(other[...])).astype(jnp.bfloat16)

    def step_RA(n):
        for q in range(4):
            got(("p", n, q))
            acc[q, pl.ds(n * 4, 4)] = (
                wide(part[pl.ds(n * 4, 4), :, cols(q, c)]) + wide(from_mate[q, pl.ds(n * 4, 4)])
            ).astype(jnp.bfloat16)
        if RETURN_MODES[n]:
            ev["ry", n] = net.send(
                acc.at[pl.ds(0, 4), pl.ds(n * 4 + (1 - k) * 2, 2)], from_y.at[n], to_y
            )
        else:
            ev["ar", n] = net.send(acc.at[far, pl.ds(n * 4, 2)], hop_a.at[n, 0], to_right)
            ev["al", n] = net.send(acc.at[far, pl.ds(n * 4 + 2, 2)], hop_a.at[n, 1], to_left)

    def step_RY(n):
        got(("ry", n))
        own = n * 4 + k * 2
        add(acc.at[pl.ds(0, 4), pl.ds(own, 2)], from_y.at[n])
        ev["ar", n] = net.send(acc.at[far, pl.ds(own, 1)], hop_a.at[n, 0, pl.ds(0, 1)], to_right)
        ev["al", n] = net.send(acc.at[far, pl.ds(own + 1, 1)], hop_a.at[n, 1, pl.ds(0, 1)], to_left)

    def step_RB(n):
        got(("ar", n))
        if RETURN_MODES[n]:
            own = n * 4 + k * 2
            add(acc.at[right, pl.ds(own, 1)], hop_a.at[n, 0, pl.ds(0, 1)])
            ev["br", n] = net.send(acc.at[right, pl.ds(own, 2)], hop_b.at[n, 0, pl.ds(0, 2)], to_right)
        else:
            add(acc.at[right, pl.ds(n * 4, 2)], hop_a.at[n, 0])
            ev["br", n] = net.send(acc.at[right, pl.ds(n * 4, 4)], hop_b.at[n, 0], to_right)

    def step_RX(n):
        got(("al", n))
        if RETURN_MODES[n]:
            own = n * 4 + k * 2
            add(acc.at[left, pl.ds(own + 1, 1)], hop_a.at[n, 1, pl.ds(0, 1)])
            ev["bl", n] = net.send(acc.at[left, pl.ds(own, 2)], hop_b.at[n, 1, pl.ds(0, 2)], to_left)
        else:
            add(acc.at[left, pl.ds(n * 4 + 2, 2)], hop_a.at[n, 1])
            ev["bl", n] = net.send(acc.at[left, pl.ds(n * 4, 4)], hop_b.at[n, 1], to_left)

    def step_RC(n):
        got(("br", n), ("bl", n))
        block, count = (n * 4 + k * 2, 2) if RETURN_MODES[n] else (n * 4, 4)
        ref = acc.at[x, pl.ds(block, count)]
        ref[...] = (
            wide(ref[...]) + wide(hop_b[n, 0, pl.ds(0, count)]) + wide(hop_b[n, 1, pl.ds(0, count)])
        ).astype(jnp.bfloat16)
        if RETURN_MODES[n]:
            give_back(n)
        else:
            ev["ry", n] = net.send(
                acc.at[x, pl.ds(n * 4 + (1 - k) * 2, 2)], from_y.at[n, 0], to_y
            )

    def step_RD(n):
        got(("ry", n))
        add(acc.at[x, pl.ds(n * 4 + k * 2, 2)], from_y.at[n, 0])
        give_back(n)

    me = z * 2 + y // 2

    def give_back(n):
        zs = (z + Z - NEAR[n]) % Z
        for j in range(2):
            src = acc.at[x, n * 4 + k * 2 + (y // 2 if j == 0 else 1 - y // 2)]
            if n == 0 and j == 0:
                ev["own_back"] = pltpu.make_async_copy(src, slots.at[me], own_sem.at[3])
                ev["own_back"].start()
            else:
                ev["back", n, j] = net.send(
                    src, slots.at[me], device(zs, y if j == 0 else 3 - y, c, x)
                )

    stores = {"GU": [], "GD": []}

    def store(name, i, src, dst):
        copy = pltpu.make_async_copy(src, dst, tile_sem.at[0 if name == "GU" else 1, i % 2])
        copy.start()
        stores[name].append(copy)

    def step_GU(i):
        if i >= 2:
            stores["GU"][i - 2].wait()
        tile = xy[0, :, :, i * TILE : (i + 1) * TILE].reshape(ROWS, TILE)
        tile_up[i % 2] = lax.dot_general(
            tile, d_pre[...], (((0,), (0,)), ((), ())), preferred_element_type=jnp.float32
        )
        store("GU", i, tile_up.at[i % 2], grad_up.at[pl.ds(i * TILE, TILE)])

    def step_GD(i):
        if i >= 2:
            stores["GD"][i - 2].wait()
        tile = xy[1, :, :, i * TILE : (i + 1) * TILE].reshape(ROWS, TILE)
        tile_down[i % 2] = lax.dot_general(
            act[...], tile, (((0,), (0,)), ((), ())), preferred_element_type=jnp.float32
        )
        store("GD", i, tile_down.at[i % 2], grad_down.at[:, pl.ds(i * TILE, TILE)])

    steps = dict(
        A=step_A, B=step_B, Br=step_Br, Bl=step_Bl, Cr=step_Cr, Cl=step_Cl, C=step_C, D=step_D,
        F=step_F, RA=step_RA, RY=step_RY, RB=step_RB, RX=step_RX, RC=step_RC, RD=step_RD,
        GU=step_GU, GD=step_GD,
    )
    for name in ORDER:
        steps[name[:-1]](int(name[-1]))

    for key in list(ev):
        if key[0] == "back":
            got(key)
    ev["own_back"].wait()
    combined = jnp.zeros((2 * TOK, HALF), jnp.float32)
    back = slots[...].reshape(EXPERTS * PAIR, HALF)

    def combine(s):
        return lax.dot_general(
            sel[s], back, (((0,), (0,)), ((), ())), preferred_element_type=jnp.float32
        ).astype(jnp.bfloat16)

    result[0] = combine(1 - c)
    last = net.send(result.at[0], final, mate)
    result[1] = combine(c)
    last.wait_recv()

    @pl.when(c == 0)
    def _():
        out[:, 0:HALF] = result[1]
        out[:, HALF:QUARTER] = final[...]

    @pl.when(c == 1)
    def _():
        out[:, 0:HALF] = final[...]
        out[:, HALF:QUARTER] = result[1]

    for name in ("GU", "GD"):
        for copy in stores[name][-2:]:
            copy.wait()
    net.finish()


def local(tokens, grad_out, routes, gates, w_up, w_down):
    bf16, f32 = jnp.bfloat16, jnp.float32
    inside = pl.BlockSpec(memory_space=pltpu.VMEM)
    anywhere = pl.BlockSpec(memory_space=pl.ANY)
    return pl.pallas_call(
        kernel,
        out_shape=(
            jax.ShapeDtypeStruct((TOK, QUARTER), bf16),
            jax.ShapeDtypeStruct((D, HID_DEV), f32),
            jax.ShapeDtypeStruct((HID_DEV, D), f32),
        ),
        in_specs=[inside] * 4 + [anywhere] * 2,
        out_specs=(inside, anywhere, anywhere),
        scratch_shapes=[
            pltpu.VMEM((2, TOK), jnp.int32),
            pltpu.VMEM((2, TOK), f32),
            pltpu.VMEM((TOK, QUARTER), bf16),
            pltpu.VMEM((2, EXPERTS * PAIR, TOK), bf16),
            pltpu.VMEM((EXPERTS, PAIR, QUARTER), bf16),
            pltpu.VMEM((2, BLOCKS, PAIR, D), bf16),
            pltpu.VMEM((D, HID_DEV), bf16),
            pltpu.VMEM((HID_DEV, D), bf16),
            pltpu.VMEM((ROWS, HID_DEV), bf16),
            pltpu.VMEM((ROWS, HID_DEV), bf16),
            pltpu.VMEM((BLOCKS, PAIR, D), bf16),
            pltpu.VMEM((4, BLOCKS, PAIR, HALF), bf16),
            pltpu.VMEM((4, BLOCKS, PAIR, HALF), bf16),
            pltpu.VMEM((Z, 2, 2, PAIR, HALF), bf16),
            pltpu.VMEM((Z, 2, 4, PAIR, HALF), bf16),
            pltpu.VMEM((Z, 4, 2, PAIR, HALF), bf16),
            pltpu.VMEM((EXPERTS, PAIR, HALF), bf16),
            pltpu.VMEM((2, TOK, HALF), bf16),
            pltpu.VMEM((TOK, HALF), bf16),
            pltpu.VMEM((2, TILE, HID_DEV), f32),
            pltpu.VMEM((2, HID_DEV, TILE), f32),
            pltpu.SemaphoreType.DMA((224,)),
            pltpu.SemaphoreType.DMA((224,)),
            pltpu.SemaphoreType.DMA((4,)),
            pltpu.SemaphoreType.DMA((2, 2)),
        ],
        compiler_params=pltpu.CompilerParams(
            collective_id=0, has_side_effects=True, vmem_limit_bytes=60 * 1024 * 1024
        ),
        name="expert_backward",
    )(routes.T, gates.T, tokens, grad_out, w_up, w_down)


def solution(mesh):
    return jax.shard_map(
        local,
        mesh=mesh,
        in_specs=(
            P("expert", "tensor"),
            P("expert", "tensor"),
            P("expert", None),
            P("expert", None),
            P(None, ("expert", "tensor")),
            P(("expert", "tensor"), None),
        ),
        out_specs=(
            P("expert", "tensor"),
            P(None, ("expert", "tensor")),
            P(("expert", "tensor"), None),
        ),
        check_vma=False,
    )
```

```python
import jax
import jax.numpy as jnp
from jax import lax
from jax.experimental import pallas as pl
from jax.experimental.pallas import tpu as pltpu
from jax.sharding import PartitionSpec as P

MESH = pl.DeviceIdType.MESH
Z, Y, X = 8, 4, 4
CAP, PAIR = 20, 40
EXPERTS = 16
BLOCKS = 32
ROWS = BLOCKS * PAIR
TOK = 128
QUARTER = 512
HALF = 256
D = 2048
HID_DEV = 512
TILE = 256
PARTS = 4
VMEM_MIB = 46
NEAR = (0, 1, 7, 2, 6, 3, 5, 4)
MODES = (1, 0, 0, 1, 0, 0, 1, 0)
RETURN_MODES = (1, 0, 1, 0, 1, 0, 0, 0)
GROUPS = ((0, 1), (2, 3), (4, 5), (6, 7))
ORDER = (
    "A0", "A1", "A2", "Br0", "Bl0", "B1", "A3", "A4", "B2", "C0", "Cr1", "Cl1", "Br3", "Bl3", "A5",
    "A6", "B4", "Cr2", "Cl2", "A7", "D0", "D1", "C3", "F0", "B5", "Br6", "Bl6", "Cr4", "Cl4", "RA0",
    "D2", "B7", "RA1", "D3", "Cr5", "Cl5", "F1", "D4", "C6", "Cr7", "Cl7", "RA2", "RY0", "RB1",
    "RX1", "RA3", "D5", "D6", "D7", "RB0", "RX0", "F2", "RC1", "RY2", "RB3", "RX3", "F3", "RC0",
    "RB2", "RX2", "RA4", "RA5", "GU0", "RC3", "RA6", "GD0", "RA7", "RC2", "GU1", "RB5", "RX5",
    "GD1", "GU2", "RB6", "RX6", "GD2", "RY4", "RB7", "RX7", "GU3", "GD3", "RC5", "GU4", "GD4",
    "GU5", "RB4", "RX4", "RC6", "GD5", "GU6", "GD6", "RC7", "GU7", "RC4", "GD7",
)

root_half = 0.7071067811865476
gauss_norm = 0.3989422804014327


def gelu_value(v):
    return 0.5 * v * (1.0 + lax.erf(v * root_half))


def gelu_slope(v):
    return 0.5 * (1.0 + lax.erf(v * root_half)) + v * jnp.exp(-0.5 * v * v) * gauss_norm


def place():
    e = lax.axis_index("expert")
    x = lax.axis_index("tensor")
    return e // 8, (e // 2) % 4, e % 2, x


def device(z, y, c, x):
    return ((z * Y + y) * 2 + c, x)


class Net:
    def __init__(self, send_sem, recv_sem):
        self.send_sem, self.recv_sem, self.count, self.sent = send_sem, recv_sem, 0, []

    def make(self, src, dst, target):
        i = self.count
        self.count += 1
        copy = pltpu.make_async_remote_copy(
            src_ref=src,
            dst_ref=dst,
            send_sem=self.send_sem.at[i],
            recv_sem=self.recv_sem.at[i],
            device_id=target,
            device_id_type=MESH,
        )
        self.sent.append(copy)
        return copy

    def send(self, src, dst, target):
        copy = self.make(src, dst, target)
        copy.start()
        return copy

    def finish(self):
        for copy in self.sent:
            copy.wait_send()


def kernel(
    routes, gates, tok, grad, w_up, w_down,
    out, grad_up, grad_down,
    route_buf, gate_buf, values, sel, send_slots, xy, wu, wd, act, d_pre, part, from_mate, acc,
    hop_a, hop_b, from_y, slots, result, final,
    send_sem, recv_sem, own_sem,
):
    z, y, c, x = place()
    k = ((y + 1) // 2) % 2
    partner = y + 1 - 2 * (y % 2)
    net = Net(send_sem, recv_sem)
    mate = device(z, y, 1 - c, x)
    right, left, far = (x + 1) % X, (x + 3) % X, (x + 2) % X
    to_right, to_left = device(z, y, c, right), device(z, y, c, left)
    to_y = device(z, partner, c, x)

    slots[...] = jnp.zeros_like(slots)
    others = [mate, to_right, to_left]
    for dz in NEAR[::-1]:
        for row in (3 - partner, 3 - y, partner, y):
            if dz or row is not y:
                others.append(device((z + dz) % Z, row, c, x))
    barrier = pltpu.get_barrier_semaphore()
    for other in others:
        pl.semaphore_signal(barrier, inc=1, device_id=other, device_id_type=MESH)

    up_copy = pltpu.make_async_copy(w_up, wu, own_sem.at[0])
    down_copy = pltpu.make_async_copy(w_down, wd, own_sem.at[1])
    up_copy.start()
    down_copy.start()

    row = lax.broadcasted_iota(jnp.int32, (EXPERTS * PAIR, TOK), 0)
    expert = lax.broadcasted_iota(jnp.int32, (EXPERTS, TOK), 0)
    before = (
        lax.broadcasted_iota(jnp.int32, (TOK, TOK), 0)
        < lax.broadcasted_iota(jnp.int32, (TOK, TOK), 1)
    ).astype(jnp.bfloat16)

    def choose(r, g, s):
        named0 = (expert == r[0:1]).astype(jnp.float32)
        named1 = (expert == r[1:2]).astype(jnp.float32)
        earlier = jnp.dot(
            (named0 + named1).astype(jnp.bfloat16), before, preferred_element_type=jnp.float32
        )
        slot0 = jnp.sum(named0 * earlier, axis=0, keepdims=True).astype(jnp.int32)
        slot1 = jnp.sum(named1 * earlier, axis=0, keepdims=True).astype(jnp.int32)
        hit0 = row == r[0:1] * PAIR + s * CAP + slot0
        hit1 = row == r[1:2] * PAIR + s * CAP + slot1
        pick = jnp.where(hit0 | hit1, 1.0, 0.0).astype(jnp.bfloat16)
        weight = jnp.where(hit0, g[0:1], 0.0) + jnp.where(hit1, g[1:2], 0.0)
        return pick, jnp.sum(weight, axis=1, keepdims=True)

    mine = jnp.where(c == 0, tok[...], grad[...])
    pick, scale = choose(routes[...], gates[...], c)
    sel[c] = pick
    total = jnp.dot(pick, mine, preferred_element_type=jnp.float32)

    pl.semaphore_wait(barrier, len(others))
    first = net.send(routes, route_buf, mate)
    second = net.send(gates, gate_buf, mate)
    third = net.make(tok, values, mate)

    @pl.when(c == 0)
    def _():
        pltpu.make_async_remote_copy(
            src_ref=grad, dst_ref=values, send_sem=send_sem.at[2], recv_sem=recv_sem.at[2],
            device_id=mate, device_id_type=MESH,
        ).start()

    @pl.when(c == 1)
    def _():
        third.start()

    first.wait_recv()
    second.wait_recv()
    pick, more = choose(route_buf[...], gate_buf[...], 1 - c)
    sel[1 - c] = pick
    scale = scale + more
    third.wait_recv()
    total = total + jnp.dot(pick, values[...], preferred_element_type=jnp.float32)
    total = total * jnp.where(c == 0, 1.0, scale)
    send_slots[...] = total.astype(jnp.bfloat16).reshape(EXPERTS, PAIR, QUARTER)

    def cols(q, core=None):
        if core is None:
            return pl.ds(pl.multiple_of(q * QUARTER, QUARTER), QUARTER)
        return pl.ds(pl.multiple_of(q * QUARTER + core * HALF, HALF), HALF)

    ev = {}
    for n, dz in enumerate(NEAR):
        ze = (z + dz) % Z
        for j in range(2):
            src = send_slots.at[ze * 2 + (y // 2 if j == 0 else 1 - y // 2)]
            dst = xy.at[c, n * 4 + k * 2 + y // 2, :, cols(x)]
            if dz == 0 and j == 0:
                local_slots = pltpu.make_async_copy(src, dst, own_sem.at[2])
                local_slots.start()
            else:
                ev["z", n, j] = net.send(src, dst, device(ze, y if j == 0 else 3 - y, c, x))

    def share(key, block, count, q, target):
        ref = xy.at[c, pl.ds(block, count), :, cols(q)]
        ev[key] = net.send(ref, ref, target)

    def got(*keys):
        for key in keys:
            if key not in done:
                done.add(key)
                ev[key].wait_recv()

    done = set()

    def step_A(n):
        if n == 0:
            local_slots.wait()
        else:
            got(("z", n, 0))
        got(("z", n, 1))
        own = n * 4 + k * 2
        share(("r", n), own, 2, x, to_right)
        share(("l", n), own, 2, x, to_left)
        share(("y", n), own, 2, x, to_y)

    def step_B(n):
        got(("y", n))
        other = n * 4 + (1 - k) * 2
        share(("r2", n), other, 2, x, to_right)
        share(("l2", n), other, 2, x, to_left)

    def step_Cr(n):
        got(("r", n), ("r2", n))
        share(("fr", n), n * 4, 2, left, to_right)

    def step_Cl(n):
        got(("l", n), ("l2", n))
        share(("fl", n), n * 4 + 2, 2, right, to_left)

    def step_Br(n):
        got(("r", n))
        own = n * 4 + k * 2
        share(("fr", n), own, 1, left, to_right)
        share(("y1", n), own, 2, left, to_y)

    def step_Bl(n):
        got(("l", n))
        own = n * 4 + k * 2
        share(("fl", n), own + 1, 1, right, to_left)
        share(("y2", n), own, 2, right, to_y)

    def step_C(n):
        got(("fr", n), ("fl", n))
        share(("y3", n), n * 4 + k * 2, 2, far, to_y)

    def step_D(n):
        if MODES[n]:
            got(("y", n), ("y1", n), ("y2", n), ("y3", n))
        else:
            got(("fr", n), ("fl", n))
        ref = xy.at[c, pl.ds(n * 4, 4)]
        ev["m", n] = net.send(ref, ref, mate)

    def step_F(g):
        if g == 0:
            up_copy.wait()
            down_copy.wait()
        got(*[("m", n) for n in GROUPS[g]])
        first_block, count = GROUPS[g][0] * 4, len(GROUPS[g]) * 4
        rows, size = pl.ds(first_block * PAIR, count * PAIR), count * PAIR
        rows_x = xy[0, pl.ds(first_block, count)].reshape(size, D)
        rows_y = xy[1, pl.ds(first_block, count)].reshape(size, D)
        pre = jnp.dot(rows_x, wu[...], preferred_element_type=jnp.float32)
        d_act = lax.dot_general(
            rows_y, wd[...], (((1,), (1,)), ((), ())), preferred_element_type=jnp.float32
        )
        act[rows] = gelu_value(pre).astype(jnp.bfloat16)
        slope = (d_act * gelu_slope(pre)).astype(jnp.bfloat16)
        d_pre[rows] = slope
        product = lax.dot_general(
            slope, wu[...], (((1,), (1,)), ((), ())), preferred_element_type=jnp.float32
        )
        part[pl.ds(first_block, count)] = product.astype(jnp.bfloat16).reshape(count, PAIR, D)
        for n in GROUPS[g]:
            for q in range(4):
                ev["p", n, q] = net.send(
                    part.at[pl.ds(n * 4, 4), :, cols(q, 1 - c)], from_mate.at[q, pl.ds(n * 4, 4)], mate
                )

    def wide(value):
        return value.astype(jnp.float32)

    def add(ref, other):
        ref[...] = (wide(ref[...]) + wide(other[...])).astype(jnp.bfloat16)

    def step_RA(n):
        for q in range(4):
            got(("p", n, q))
            acc[q, pl.ds(n * 4, 4)] = (
                wide(part[pl.ds(n * 4, 4), :, cols(q, c)]) + wide(from_mate[q, pl.ds(n * 4, 4)])
            ).astype(jnp.bfloat16)
        if RETURN_MODES[n]:
            ev["ry", n] = net.send(
                acc.at[pl.ds(0, 4), pl.ds(n * 4 + (1 - k) * 2, 2)], from_y.at[n], to_y
            )
        else:
            ev["ar", n] = net.send(acc.at[far, pl.ds(n * 4, 2)], hop_a.at[n, 0], to_right)
            ev["al", n] = net.send(acc.at[far, pl.ds(n * 4 + 2, 2)], hop_a.at[n, 1], to_left)

    def step_RY(n):
        got(("ry", n))
        own = n * 4 + k * 2
        add(acc.at[pl.ds(0, 4), pl.ds(own, 2)], from_y.at[n])
        ev["ar", n] = net.send(acc.at[far, pl.ds(own, 1)], hop_a.at[n, 0, pl.ds(0, 1)], to_right)
        ev["al", n] = net.send(acc.at[far, pl.ds(own + 1, 1)], hop_a.at[n, 1, pl.ds(0, 1)], to_left)

    def step_RB(n):
        got(("ar", n))
        if RETURN_MODES[n]:
            own = n * 4 + k * 2
            add(acc.at[right, pl.ds(own, 1)], hop_a.at[n, 0, pl.ds(0, 1)])
            ev["br", n] = net.send(acc.at[right, pl.ds(own, 2)], hop_b.at[n, 0, pl.ds(0, 2)], to_right)
        else:
            add(acc.at[right, pl.ds(n * 4, 2)], hop_a.at[n, 0])
            ev["br", n] = net.send(acc.at[right, pl.ds(n * 4, 4)], hop_b.at[n, 0], to_right)

    def step_RX(n):
        got(("al", n))
        if RETURN_MODES[n]:
            own = n * 4 + k * 2
            add(acc.at[left, pl.ds(own + 1, 1)], hop_a.at[n, 1, pl.ds(0, 1)])
            ev["bl", n] = net.send(acc.at[left, pl.ds(own, 2)], hop_b.at[n, 1, pl.ds(0, 2)], to_left)
        else:
            add(acc.at[left, pl.ds(n * 4 + 2, 2)], hop_a.at[n, 1])
            ev["bl", n] = net.send(acc.at[left, pl.ds(n * 4, 4)], hop_b.at[n, 1], to_left)

    me = z * 2 + y // 2

    def step_RC(n):
        got(("br", n), ("bl", n))
        own = n * 4 + k * 2
        block, count = (own, 2) if RETURN_MODES[n] else (n * 4, 4)
        ref = acc.at[x, pl.ds(block, count)]
        ref[...] = (
            wide(ref[...]) + wide(hop_b[n, 0, pl.ds(0, count)]) + wide(hop_b[n, 1, pl.ds(0, count)])
        ).astype(jnp.bfloat16)
        zs = (z + Z - NEAR[n]) % Z
        other = n * 4 + (1 - k) * 2
        for j in range(2 if RETURN_MODES[n] else 4):
            row = y if j % 2 == 0 else 3 - y
            block = own if j < 2 else other
            block = block + (y // 2 if j % 2 == 0 else 1 - y // 2)
            if j >= 2:
                row = partner if j % 2 == 0 else 3 - partner
            dst = slots.at[j // 2, me]
            if n == 0 and j == 0:
                ev["own_back"] = pltpu.make_async_copy(acc.at[x, block], dst, own_sem.at[3])
                ev["own_back"].start()
            else:
                ev["back", n, j] = net.send(acc.at[x, block], dst, device(zs, row, c, x))

    def step_GU(i):
        tile = xy[0, :, :, i * TILE : (i + 1) * TILE].reshape(ROWS, TILE)
        grad_up[i * TILE : (i + 1) * TILE] = lax.dot_general(
            tile, d_pre[...], (((0,), (0,)), ((), ())), preferred_element_type=jnp.float32
        )

    def step_GD(i):
        tile = xy[1, :, :, i * TILE : (i + 1) * TILE].reshape(ROWS, TILE)
        grad_down[:, i * TILE : (i + 1) * TILE] = lax.dot_general(
            act[...], tile, (((0,), (0,)), ((), ())), preferred_element_type=jnp.float32
        )

    steps = dict(
        A=step_A, B=step_B, Br=step_Br, Bl=step_Bl, Cr=step_Cr, Cl=step_Cl, C=step_C, D=step_D,
        F=step_F, RA=step_RA, RY=step_RY, RB=step_RB, RX=step_RX, RC=step_RC,
        GU=step_GU, GD=step_GD,
    )
    for name in ORDER:
        steps[name[:-1]](int(name[-1]))

    for key in list(ev):
        if key[0] == "back":
            got(key)
    ev["own_back"].wait()
    def combine(s):
        total = jnp.zeros((TOK, HALF), jnp.float32)
        for h in range(2):
            total = total + lax.dot_general(
                sel[s],
                slots[h].reshape(EXPERTS * PAIR, HALF),
                (((0,), (0,)), ((), ())),
                preferred_element_type=jnp.float32,
            )
        return total.astype(jnp.bfloat16)

    result[0] = combine(1 - c)
    last = net.send(result.at[0], final, mate)
    result[1] = combine(c)
    last.wait_recv()

    @pl.when(c == 0)
    def _():
        out[:, 0:HALF] = result[1]
        out[:, HALF:QUARTER] = final[...]

    @pl.when(c == 1)
    def _():
        out[:, 0:HALF] = final[...]
        out[:, HALF:QUARTER] = result[1]

    net.finish()


def store_kernel(tok, up, down, tok_out, up_out, down_out, sem):
    copies = [pltpu.make_async_copy(tok, tok_out, sem.at[0])]
    for i in range(PARTS):
        for j, (src, dst) in enumerate(((up, up_out), (down, down_out))):
            size = src.shape[0] // PARTS
            rows = pl.ds(i * size, size)
            copies.append(pltpu.make_async_copy(src.at[rows], dst.at[rows], sem.at[1 + 2 * i + j]))
    for copy in copies:
        copy.start()
    for copy in copies:
        copy.wait()


def local(tokens, grad_out, routes, gates, w_up, w_down):
    bf16, f32 = jnp.bfloat16, jnp.float32
    inside = pl.BlockSpec(memory_space=pltpu.VMEM)
    anywhere = pl.BlockSpec(memory_space=pl.ANY)
    grads = pl.pallas_call(
        kernel,
        out_shape=(
            pltpu.VMEM((TOK, QUARTER), bf16),
            pltpu.VMEM((D, HID_DEV), f32),
            pltpu.VMEM((HID_DEV, D), f32),
        ),
        in_specs=[inside] * 4 + [anywhere] * 2,
        out_specs=(inside, inside, inside),
        scratch_shapes=[
            pltpu.VMEM((2, TOK), jnp.int32),
            pltpu.VMEM((2, TOK), f32),
            pltpu.VMEM((TOK, QUARTER), bf16),
            pltpu.VMEM((2, EXPERTS * PAIR, TOK), bf16),
            pltpu.VMEM((EXPERTS, PAIR, QUARTER), bf16),
            pltpu.VMEM((2, BLOCKS, PAIR, D), bf16),
            pltpu.VMEM((D, HID_DEV), bf16),
            pltpu.VMEM((HID_DEV, D), bf16),
            pltpu.VMEM((ROWS, HID_DEV), bf16),
            pltpu.VMEM((ROWS, HID_DEV), bf16),
            pltpu.VMEM((BLOCKS, PAIR, D), bf16),
            pltpu.VMEM((4, BLOCKS, PAIR, HALF), bf16),
            pltpu.VMEM((4, BLOCKS, PAIR, HALF), bf16),
            pltpu.VMEM((Z, 2, 2, PAIR, HALF), bf16),
            pltpu.VMEM((Z, 2, 4, PAIR, HALF), bf16),
            pltpu.VMEM((Z, 4, 2, PAIR, HALF), bf16),
            pltpu.VMEM((2, EXPERTS, PAIR, HALF), bf16),
            pltpu.VMEM((2, TOK, HALF), bf16),
            pltpu.VMEM((TOK, HALF), bf16),
            pltpu.SemaphoreType.DMA((224,)),
            pltpu.SemaphoreType.DMA((224,)),
            pltpu.SemaphoreType.DMA((4,)),
        ],
        compiler_params=pltpu.CompilerParams(
            collective_id=0, has_side_effects=True, vmem_limit_bytes=VMEM_MIB * 1024 * 1024
        ),
        name="expert_backward",
    )(routes.T, gates.T, tokens, grad_out, w_up, w_down)
    return pl.pallas_call(
        store_kernel,
        out_shape=tuple(jax.ShapeDtypeStruct(g.shape, g.dtype) for g in grads),
        in_specs=[inside] * 3,
        out_specs=(anywhere,) * 3,
        scratch_shapes=[pltpu.SemaphoreType.DMA((1 + 2 * PARTS,))],
        compiler_params=pltpu.CompilerParams(vmem_limit_bytes=1024 * 1024),
        name="store_grads",
    )(*grads)


def solution(mesh):
    return jax.shard_map(
        local,
        mesh=mesh,
        in_specs=(
            P("expert", "tensor"),
            P("expert", "tensor"),
            P("expert", None),
            P("expert", None),
            P(None, ("expert", "tensor")),
            P(("expert", "tensor"), None),
        ),
        out_specs=(
            P("expert", "tensor"),
            P(None, ("expert", "tensor")),
            P(("expert", "tensor"), None),
        ),
        check_vma=False,
    )
```

```python
import jax
import jax.numpy as jnp
from jax import lax
from jax.experimental import pallas as pl
from jax.experimental.pallas import tpu as pltpu
from jax.sharding import PartitionSpec as P

MESH = pl.DeviceIdType.MESH
Z, Y, X = 8, 4, 4
CAP, PAIR = 20, 40
EXPERTS = 16
BLOCKS = 32
ROWS = BLOCKS * PAIR
TOK = 128
QUARTER = 512
HALF = 256
D = 2048
HID_DEV = 512
TILE = 256
PARTS = 1
VMEM_MIB = 48
NEAR = (0, 7, 2, 6, 4, 3, 5, 1)
MODES = (1, 0, 1, 0, 0, 1, 1, 0)
RETURN_MODES = (0, 0, 2, 1, 0, 0, 1, 0)
GROUPS = ((0, 1), (2, 3), (4, 5), (6,), (7,))
ORDER = (
    "A0", "A1", "Br0", "Bl0", "A2", "B1", "A3", "C0", "Br2", "Bl2", "Cr1", "Cl1", "A4", "B3", "C2",
    "A5", "A7", "D0", "D1", "A6", "Cr3", "Cl3", "F0", "B4", "Br5", "Bl5", "D2", "RA0", "Br6", "Bl6",
    "RA1", "B7", "D3", "Cr4", "Cl4", "F1", "RB0", "RX0", "RB1", "RX1", "C5", "C6", "RA2", "Cr7",
    "Cl7", "RA3", "D4", "D5", "RC0", "D6", "RC1", "F2", "F3", "RA4", "RY3", "RA5", "RC2", "D7",
    "RA6", "RB4", "RX4", "RB3", "RX3", "F4", "RB5", "RX5", "GU0", "GD0", "RC4", "RY6", "RA7", "RC3",
    "GU1", "GD1", "GU2", "RC5", "RB6", "RX6", "GD2", "RB7", "RX7", "GU3", "GD3", "GU4", "GD4",
    "RC6", "GU5", "GD5", "RC7", "GU6", "GD6", "GU7", "GD7",
)

root_half = 0.7071067811865476
gauss_norm = 0.3989422804014327


def gelu_value(v):
    return 0.5 * v * (1.0 + lax.erf(v * root_half))


def gelu_slope(v):
    return 0.5 * (1.0 + lax.erf(v * root_half)) + v * jnp.exp(-0.5 * v * v) * gauss_norm


def place():
    e = lax.axis_index("expert")
    x = lax.axis_index("tensor")
    return e // 8, (e // 2) % 4, e % 2, x


def device(z, y, c, x):
    return ((z * Y + y) * 2 + c, x)


class Net:
    def __init__(self, send_sem, recv_sem):
        self.send_sem, self.recv_sem, self.count, self.sent = send_sem, recv_sem, 0, []

    def make(self, src, dst, target):
        i = self.count
        self.count += 1
        copy = pltpu.make_async_remote_copy(
            src_ref=src,
            dst_ref=dst,
            send_sem=self.send_sem.at[i],
            recv_sem=self.recv_sem.at[i],
            device_id=target,
            device_id_type=MESH,
        )
        self.sent.append(copy)
        return copy

    def send(self, src, dst, target):
        copy = self.make(src, dst, target)
        copy.start()
        return copy

    def finish(self):
        for copy in self.sent:
            copy.wait_send()


def kernel(
    routes, gates, tok, grad, w_up, w_down,
    out, grad_up, grad_down,
    route_buf, gate_buf, values, sel, send_slots, xy, wu, wd, act, d_pre, part, from_mate, acc,
    hop_a, hop_b, hop_c, from_y, slots, result, final,
    send_sem, recv_sem, own_sem, ready,
):
    z, y, c, x = place()
    k = ((y + 1) // 2) % 2
    partner = y + 1 - 2 * (y % 2)
    net = Net(send_sem, recv_sem)
    mate = device(z, y, 1 - c, x)
    right, left, far = (x + 1) % X, (x + 3) % X, (x + 2) % X
    to_right, to_left = device(z, y, c, right), device(z, y, c, left)
    to_y, to_far = device(z, partner, c, x), device(z, y, c, far)

    slots[...] = jnp.zeros_like(slots)
    up, down = device((z + 1) % Z, y, c, x), device((z + Z - 1) % Z, y, c, x)
    others = [mate, to_right, to_left, to_y, device(z, 3 - y, c, x), up, down]
    barrier = pltpu.get_barrier_semaphore()
    for other in others:
        pl.semaphore_signal(barrier, inc=1, device_id=other, device_id_type=MESH)

    up_copy = pltpu.make_async_copy(w_up, wu, own_sem.at[0])
    down_copy = pltpu.make_async_copy(w_down, wd, own_sem.at[1])
    up_copy.start()
    down_copy.start()

    row = lax.broadcasted_iota(jnp.int32, (EXPERTS * PAIR, TOK), 0)
    expert = lax.broadcasted_iota(jnp.int32, (EXPERTS, TOK), 0)
    before = (
        lax.broadcasted_iota(jnp.int32, (TOK, TOK), 0)
        < lax.broadcasted_iota(jnp.int32, (TOK, TOK), 1)
    ).astype(jnp.bfloat16)

    def choose(r, g, s):
        named0 = (expert == r[0:1]).astype(jnp.float32)
        named1 = (expert == r[1:2]).astype(jnp.float32)
        earlier = jnp.dot(
            (named0 + named1).astype(jnp.bfloat16), before, preferred_element_type=jnp.float32
        )
        slot0 = jnp.sum(named0 * earlier, axis=0, keepdims=True).astype(jnp.int32)
        slot1 = jnp.sum(named1 * earlier, axis=0, keepdims=True).astype(jnp.int32)
        hit0 = row == r[0:1] * PAIR + s * CAP + slot0
        hit1 = row == r[1:2] * PAIR + s * CAP + slot1
        pick = jnp.where(hit0 | hit1, 1.0, 0.0).astype(jnp.bfloat16)
        weight = jnp.where(hit0, g[0:1], 0.0) + jnp.where(hit1, g[1:2], 0.0)
        return pick, jnp.sum(weight, axis=1, keepdims=True)

    mine = jnp.where(c == 0, tok[...], grad[...])
    pick, scale = choose(routes[...], gates[...], c)
    sel[c] = pick
    total = jnp.dot(pick, mine, preferred_element_type=jnp.float32)

    pl.semaphore_wait(barrier, len(others))

    def announce(r):
        pl.semaphore_signal(ready.at[r, 0], inc=1, device_id=up, device_id_type=MESH)
        pl.semaphore_signal(ready.at[r, 1], inc=1, device_id=down, device_id_type=MESH)

    def hear(r):
        pl.semaphore_wait(ready.at[r, 0], 1)
        pl.semaphore_wait(ready.at[r, 1], 1)

    announce(0)
    first = net.send(routes, route_buf, mate)
    second = net.send(gates, gate_buf, mate)
    third = net.make(tok, values, mate)

    @pl.when(c == 0)
    def _():
        pltpu.make_async_remote_copy(
            src_ref=grad, dst_ref=values, send_sem=send_sem.at[2], recv_sem=recv_sem.at[2],
            device_id=mate, device_id_type=MESH,
        ).start()

    @pl.when(c == 1)
    def _():
        third.start()

    first.wait_recv()
    second.wait_recv()
    hear(0)
    announce(1)
    pick, more = choose(route_buf[...], gate_buf[...], 1 - c)
    sel[1 - c] = pick
    scale = scale + more
    hear(1)
    announce(2)
    third.wait_recv()
    total = total + jnp.dot(pick, values[...], preferred_element_type=jnp.float32)
    total = total * jnp.where(c == 0, 1.0, scale)
    send_slots[...] = total.astype(jnp.bfloat16).reshape(EXPERTS, PAIR, QUARTER)

    def cols(q):
        return pl.ds(pl.multiple_of(q * QUARTER, QUARTER), QUARTER)

    ev = {}
    own_block = xy.at[c, k * 2 + y // 2, :, cols(x)]
    own_slots = send_slots.at[z * 2 + y // 2]
    ev["r", 0, "a"] = net.send(own_slots, own_block, to_right)
    ev["l", 0, "a"] = net.send(own_slots, own_block, to_left)
    ev["y", 0, "a"] = net.send(own_slots, own_block, to_y)
    heard = 2
    for n, dz in enumerate(NEAR):
        while heard < min(dz, Z - dz):
            hear(heard)
            heard += 1
            if heard < 4:
                announce(heard)
        ze = (z + dz) % Z
        for j in range(2):
            src = send_slots.at[ze * 2 + (y // 2 if j == 0 else 1 - y // 2)]
            dst = xy.at[c, n * 4 + k * 2 + y // 2, :, cols(x)]
            if dz == 0 and j == 0:
                local_slots = pltpu.make_async_copy(src, dst, own_sem.at[2])
                local_slots.start()
            else:
                ev["z", n, j] = net.send(src, dst, device(ze, y if j == 0 else 3 - y, c, x))

    def share(key, block, count, q, target):
        ref = xy.at[c, pl.ds(block, count), :, cols(q)]
        ev[key] = net.send(ref, ref, target)

    def got(*keys):
        for name in keys:
            for key in (name, name + ("a",)):
                if key in ev and key not in done:
                    done.add(key)
                    ev[key].wait_recv()

    done = set()

    def step_A(n):
        if n == 0:
            local_slots.wait()
        else:
            got(("z", n, 0))
        got(("z", n, 1))
        own, count = (k * 2 + 1 - y // 2, 1) if n == 0 else (n * 4 + k * 2, 2)
        share(("r", n), own, count, x, to_right)
        share(("l", n), own, count, x, to_left)
        share(("y", n), own, count, x, to_y)

    def step_B(n):
        got(("y", n))
        other = n * 4 + (1 - k) * 2
        share(("r2", n), other, 2, x, to_right)
        share(("l2", n), other, 2, x, to_left)

    def step_Cr(n):
        got(("r", n), ("r2", n))
        share(("fr", n), n * 4, 2, left, to_right)

    def step_Cl(n):
        got(("l", n), ("l2", n))
        share(("fl", n), n * 4 + 2, 2, right, to_left)

    def step_Br(n):
        got(("r", n))
        own = n * 4 + k * 2
        share(("fr", n), own, 1, left, to_right)
        share(("y1", n), own, 2, left, to_y)

    def step_Bl(n):
        got(("l", n))
        own = n * 4 + k * 2
        share(("fl", n), own + 1, 1, right, to_left)
        share(("y2", n), own, 2, right, to_y)

    def step_C(n):
        got(("fr", n), ("fl", n))
        share(("y3", n), n * 4 + k * 2, 2, far, to_y)

    def step_D(n):
        if MODES[n]:
            got(("y", n), ("y1", n), ("y2", n), ("y3", n))
        else:
            got(("fr", n), ("fl", n))
        ref = xy.at[c, pl.ds(n * 4, 4)]
        ev["m", n] = net.send(ref, ref, mate)

    def step_F(g):
        if g == 0:
            up_copy.wait()
            down_copy.wait()
        got(*[("m", n) for n in GROUPS[g]])
        first_block, count = GROUPS[g][0] * 4, len(GROUPS[g]) * 4
        rows, size = pl.ds(first_block * PAIR, count * PAIR), count * PAIR
        rows_x = xy[0, pl.ds(first_block, count)].reshape(size, D)
        rows_y = xy[1, pl.ds(first_block, count)].reshape(size, D)
        pre = jnp.dot(rows_x, wu[...], preferred_element_type=jnp.float32)
        d_act = lax.dot_general(
            rows_y, wd[...], (((1,), (1,)), ((), ())), preferred_element_type=jnp.float32
        )
        act[rows] = gelu_value(pre).astype(jnp.bfloat16)
        slope = (d_act * gelu_slope(pre)).astype(jnp.bfloat16)
        d_pre[rows] = slope
        product = lax.dot_general(
            slope, wu[...], (((1,), (1,)), ((), ())), preferred_element_type=jnp.float32
        )
        for q in range(4):
            for h in range(2):
                at = q * QUARTER + h * HALF
                part[h, q, pl.ds(first_block, count)] = (
                    product[:, at : at + HALF].astype(jnp.bfloat16).reshape(count, PAIR, HALF)
                )
        for n in GROUPS[g]:
            ev["p", n] = net.send(
                part.at[1 - c, :, pl.ds(n * 4, 4)], from_mate.at[:, pl.ds(n * 4, 4)], mate
            )

    def wide(value):
        return value.astype(jnp.float32)

    def add(ref, other):
        ref[...] = (wide(ref[...]) + wide(other[...])).astype(jnp.bfloat16)

    def step_RA(n):
        got(("p", n))
        for q in range(4):
            acc[q, pl.ds(n * 4, 4)] = (
                wide(part[c, q, pl.ds(n * 4, 4)]) + wide(from_mate[q, pl.ds(n * 4, 4)])
            ).astype(jnp.bfloat16)
        if RETURN_MODES[n] == 2:
            ev["br", n] = net.send(acc.at[right, pl.ds(n * 4, 4)], hop_b.at[n, 0], to_right)
            ev["bl", n] = net.send(acc.at[left, pl.ds(n * 4, 4)], hop_b.at[n, 1], to_left)
            ev["far", n] = net.send(acc.at[far, pl.ds(n * 4, 4)], hop_c.at[n], to_far)
        elif RETURN_MODES[n] == 1:
            ev["ry", n] = net.send(
                acc.at[pl.ds(0, 4), pl.ds(n * 4 + (1 - k) * 2, 2)], from_y.at[n], to_y
            )
        else:
            ev["ar", n] = net.send(acc.at[far, pl.ds(n * 4, 2)], hop_a.at[n, 0], to_right)
            ev["al", n] = net.send(acc.at[far, pl.ds(n * 4 + 2, 2)], hop_a.at[n, 1], to_left)

    def step_RY(n):
        got(("ry", n))
        own = n * 4 + k * 2
        add(acc.at[pl.ds(0, 4), pl.ds(own, 2)], from_y.at[n])
        ev["ar", n] = net.send(acc.at[far, pl.ds(own, 1)], hop_a.at[n, 0, pl.ds(0, 1)], to_right)
        ev["al", n] = net.send(acc.at[far, pl.ds(own + 1, 1)], hop_a.at[n, 1, pl.ds(0, 1)], to_left)

    def step_RB(n):
        got(("ar", n))
        if RETURN_MODES[n]:
            own = n * 4 + k * 2
            add(acc.at[right, pl.ds(own, 1)], hop_a.at[n, 0, pl.ds(0, 1)])
            ev["br", n] = net.send(acc.at[right, pl.ds(own, 2)], hop_b.at[n, 0, pl.ds(0, 2)], to_right)
        else:
            add(acc.at[right, pl.ds(n * 4, 2)], hop_a.at[n, 0])
            ev["br", n] = net.send(acc.at[right, pl.ds(n * 4, 4)], hop_b.at[n, 0], to_right)

    def step_RX(n):
        got(("al", n))
        if RETURN_MODES[n]:
            own = n * 4 + k * 2
            add(acc.at[left, pl.ds(own + 1, 1)], hop_a.at[n, 1, pl.ds(0, 1)])
            ev["bl", n] = net.send(acc.at[left, pl.ds(own, 2)], hop_b.at[n, 1, pl.ds(0, 2)], to_left)
        else:
            add(acc.at[left, pl.ds(n * 4 + 2, 2)], hop_a.at[n, 1])
            ev["bl", n] = net.send(acc.at[left, pl.ds(n * 4, 4)], hop_b.at[n, 1], to_left)

    me = z * 2 + y // 2

    def step_RC(n):
        got(("br", n), ("bl", n))
        own = n * 4 + k * 2
        single = RETURN_MODES[n] == 1
        block, count = (own, 2) if single else (n * 4, 4)
        ref = acc.at[x, pl.ds(block, count)]
        total = (
            wide(ref[...]) + wide(hop_b[n, 0, pl.ds(0, count)]) + wide(hop_b[n, 1, pl.ds(0, count)])
        )
        if RETURN_MODES[n] == 2:
            got(("far", n))
            total = total + wide(hop_c[n])
        ref[...] = total.astype(jnp.bfloat16)
        zs = (z + Z - NEAR[n]) % Z
        other = n * 4 + (1 - k) * 2
        for j in range(2 if single else 4):
            row = y if j % 2 == 0 else 3 - y
            block = own if j < 2 else other
            block = block + (y // 2 if j % 2 == 0 else 1 - y // 2)
            if j >= 2:
                row = partner if j % 2 == 0 else 3 - partner
            dst = slots.at[j // 2, me]
            if n == 0 and j == 0:
                ev["own_back"] = pltpu.make_async_copy(acc.at[x, block], dst, own_sem.at[3])
                ev["own_back"].start()
            else:
                ev["back", n, j] = net.send(acc.at[x, block], dst, device(zs, row, c, x))

    def step_GU(i):
        tile = xy[0, :, :, i * TILE : (i + 1) * TILE].reshape(ROWS, TILE)
        grad_up[i * TILE : (i + 1) * TILE] = lax.dot_general(
            tile, d_pre[...], (((0,), (0,)), ((), ())), preferred_element_type=jnp.float32
        )

    def step_GD(i):
        tile = xy[1, :, :, i * TILE : (i + 1) * TILE].reshape(ROWS, TILE)
        grad_down[:, i * TILE : (i + 1) * TILE] = lax.dot_general(
            act[...], tile, (((0,), (0,)), ((), ())), preferred_element_type=jnp.float32
        )

    steps = dict(
        A=step_A, B=step_B, Br=step_Br, Bl=step_Bl, Cr=step_Cr, Cl=step_Cl, C=step_C, D=step_D,
        F=step_F, RA=step_RA, RY=step_RY, RB=step_RB, RX=step_RX, RC=step_RC,
        GU=step_GU, GD=step_GD,
    )
    for name in ORDER:
        steps[name[:-1]](int(name[-1]))

    for key in list(ev):
        if key[0] == "back":
            got(key)
    ev["own_back"].wait()
    def combine(s):
        total = jnp.zeros((TOK, HALF), jnp.float32)
        for h in range(2):
            total = total + lax.dot_general(
                sel[s],
                slots[h].reshape(EXPERTS * PAIR, HALF),
                (((0,), (0,)), ((), ())),
                preferred_element_type=jnp.float32,
            )
        return total.astype(jnp.bfloat16)

    result[0] = combine(1 - c)
    last = net.send(result.at[0], final, mate)
    result[1] = combine(c)
    last.wait_recv()

    @pl.when(c == 0)
    def _():
        out[:, 0:HALF] = result[1]
        out[:, HALF:QUARTER] = final[...]

    @pl.when(c == 1)
    def _():
        out[:, 0:HALF] = final[...]
        out[:, HALF:QUARTER] = result[1]

    net.finish()


def store_kernel(tok, up, down, tok_out, up_out, down_out, sem):
    copies = [pltpu.make_async_copy(tok, tok_out, sem.at[0])]
    for i in range(PARTS):
        for j, (src, dst) in enumerate(((up, up_out), (down, down_out))):
            size = src.shape[0] // PARTS
            rows = pl.ds(i * size, size)
            copies.append(pltpu.make_async_copy(src.at[rows], dst.at[rows], sem.at[1 + 2 * i + j]))
    for copy in copies:
        copy.start()
    for copy in copies:
        copy.wait()


def local(tokens, grad_out, routes, gates, w_up, w_down):
    bf16, f32 = jnp.bfloat16, jnp.float32
    inside = pl.BlockSpec(memory_space=pltpu.VMEM)
    anywhere = pl.BlockSpec(memory_space=pl.ANY)
    grads = pl.pallas_call(
        kernel,
        out_shape=(
            pltpu.VMEM((TOK, QUARTER), bf16),
            pltpu.VMEM((D, HID_DEV), f32),
            pltpu.VMEM((HID_DEV, D), f32),
        ),
        in_specs=[inside] * 4 + [anywhere] * 2,
        out_specs=(inside, inside, inside),
        scratch_shapes=[
            pltpu.VMEM((2, TOK), jnp.int32),
            pltpu.VMEM((2, TOK), f32),
            pltpu.VMEM((TOK, QUARTER), bf16),
            pltpu.VMEM((2, EXPERTS * PAIR, TOK), bf16),
            pltpu.VMEM((EXPERTS, PAIR, QUARTER), bf16),
            pltpu.VMEM((2, BLOCKS, PAIR, D), bf16),
            pltpu.VMEM((D, HID_DEV), bf16),
            pltpu.VMEM((HID_DEV, D), bf16),
            pltpu.VMEM((ROWS, HID_DEV), bf16),
            pltpu.VMEM((ROWS, HID_DEV), bf16),
            pltpu.VMEM((2, 4, BLOCKS, PAIR, HALF), bf16),
            pltpu.VMEM((4, BLOCKS, PAIR, HALF), bf16),
            pltpu.VMEM((4, BLOCKS, PAIR, HALF), bf16),
            pltpu.VMEM((Z, 2, 2, PAIR, HALF), bf16),
            pltpu.VMEM((Z, 2, 4, PAIR, HALF), bf16),
            pltpu.VMEM((Z, 4, PAIR, HALF), bf16),
            pltpu.VMEM((Z, 4, 2, PAIR, HALF), bf16),
            pltpu.VMEM((2, EXPERTS, PAIR, HALF), bf16),
            pltpu.VMEM((2, TOK, HALF), bf16),
            pltpu.VMEM((TOK, HALF), bf16),
            pltpu.SemaphoreType.DMA((224,)),
            pltpu.SemaphoreType.DMA((224,)),
            pltpu.SemaphoreType.DMA((4,)),
            pltpu.SemaphoreType.REGULAR((4, 2)),
        ],
        compiler_params=pltpu.CompilerParams(
            collective_id=0, has_side_effects=True, vmem_limit_bytes=VMEM_MIB * 1024 * 1024
        ),
        name="expert_backward",
    )(routes.T, gates.T, tokens, grad_out, w_up, w_down)
    return pl.pallas_call(
        store_kernel,
        out_shape=tuple(jax.ShapeDtypeStruct(g.shape, g.dtype) for g in grads),
        in_specs=[inside] * 3,
        out_specs=(anywhere,) * 3,
        scratch_shapes=[pltpu.SemaphoreType.DMA((1 + 2 * PARTS,))],
        compiler_params=pltpu.CompilerParams(vmem_limit_bytes=1024 * 1024),
        name="store_grads",
    )(*grads)


def solution(mesh):
    return jax.shard_map(
        local,
        mesh=mesh,
        in_specs=(
            P("expert", "tensor"),
            P("expert", "tensor"),
            P("expert", None),
            P("expert", None),
            P(None, ("expert", "tensor")),
            P(("expert", "tensor"), None),
        ),
        out_specs=(
            P("expert", "tensor"),
            P(None, ("expert", "tensor")),
            P(("expert", "tensor"), None),
        ),
        check_vma=False,
    )
```

```python
import jax
import jax.numpy as jnp
from jax import lax
from jax.experimental import pallas as pl
from jax.experimental.pallas import tpu as pltpu
from jax.sharding import PartitionSpec as P

MESH = pl.DeviceIdType.MESH
Z, Y, X = 8, 4, 4
CAP, PAIR = 20, 40
EXPERTS = 16
BLOCKS = 32
ROWS = BLOCKS * PAIR
TOK = 128
QUARTER = 512
HALF = 256
D = 2048
HID_DEV = 512
TILE = 256
PARTS = 1
VMEM_MIB = 48
NEAR = (0, 1, 7, 4, 3, 5, 2, 6)
MODES = (0, 1, 0, 1, 0, 0, 0, 1)
RETURN_MODES = (1, 0, 1, 2, 0, 0, 0, 1)
GROUPS = ((0, 1), (2, 3), (4, 5), (6, 7))
ORDER = (
    "A0", "A1", "A2", "B0", "Br1", "Bl1", "A3", "B2", "Cr0", "Cl0", "C1", "Br3", "Bl3", "A4", "A5",
    "Cr2", "Cl2", "D1", "A6", "A7", "D0", "C3", "F0", "B4", "D2", "B5", "RA0", "B6", "RA1", "Br7",
    "Bl7", "Cr4", "Cl4", "D3", "Cr5", "Cl5", "F1", "RY0", "Cr6", "Cl6", "RB1", "RX1", "C7", "D4",
    "RA2", "RA3", "D5", "D7", "RB0", "RX0", "D6", "F2", "RC1", "RY2", "F3", "RA4", "RA5", "GU0",
    "RC0", "RC3", "RB2", "RX2", "GD0", "RA6", "RA7", "GU1", "GD1", "RB4", "RX4", "GU2", "RB5",
    "RX5", "GD2", "RC2", "GU3", "RB6", "RX6", "GD3", "GU4", "RC4", "RY7", "RC5", "RB7", "RX7",
    "RC6", "RC7", "GD4", "GU5", "GD5", "GU6", "GD6", "GU7", "GD7",
)

root_half = 0.7071067811865476
gauss_norm = 0.3989422804014327


def gelu_value(v):
    return 0.5 * v * (1.0 + lax.erf(v * root_half))


def gelu_slope(v):
    return 0.5 * (1.0 + lax.erf(v * root_half)) + v * jnp.exp(-0.5 * v * v) * gauss_norm


def place():
    e = lax.axis_index("expert")
    x = lax.axis_index("tensor")
    return e // 8, (e // 2) % 4, e % 2, x


def device(z, y, c, x):
    return ((z * Y + y) * 2 + c, x)


class Net:
    def __init__(self, send_sem, recv_sem):
        self.send_sem, self.recv_sem, self.count, self.sent = send_sem, recv_sem, 0, []

    def make(self, src, dst, target):
        i = self.count
        self.count += 1
        copy = pltpu.make_async_remote_copy(
            src_ref=src,
            dst_ref=dst,
            send_sem=self.send_sem.at[i],
            recv_sem=self.recv_sem.at[i],
            device_id=target,
            device_id_type=MESH,
        )
        self.sent.append(copy)
        return copy

    def send(self, src, dst, target):
        copy = self.make(src, dst, target)
        copy.start()
        return copy

    def finish(self):
        for copy in self.sent:
            copy.wait_send()


def kernel(
    routes, gates, tok, grad, w_up, w_down,
    out, grad_up, grad_down,
    route_buf, gate_buf, values, sel, send_slots, xy, wu, wd, act, d_pre, part, from_mate, acc,
    hop_a, hop_b, hop_c, from_y, slots, result, final,
    send_sem, recv_sem, own_sem, ready,
):
    z, y, c, x = place()
    k = ((y + 1) // 2) % 2
    partner = y + 1 - 2 * (y % 2)
    net = Net(send_sem, recv_sem)
    mate = device(z, y, 1 - c, x)
    right, left, far = (x + 1) % X, (x + 3) % X, (x + 2) % X
    to_right, to_left = device(z, y, c, right), device(z, y, c, left)
    to_y, to_far = device(z, partner, c, x), device(z, y, c, far)

    slots[...] = jnp.zeros_like(slots)
    up, down = device((z + 1) % Z, y, c, x), device((z + Z - 1) % Z, y, c, x)
    others = [mate, to_right, to_left, to_y, device(z, 3 - y, c, x), up, down]
    barrier = pltpu.get_barrier_semaphore()
    for other in others:
        pl.semaphore_signal(barrier, inc=1, device_id=other, device_id_type=MESH)

    up_copy = pltpu.make_async_copy(w_up, wu, own_sem.at[0])
    down_copy = pltpu.make_async_copy(w_down, wd, own_sem.at[1])
    up_copy.start()
    down_copy.start()

    row = lax.broadcasted_iota(jnp.int32, (EXPERTS * PAIR, TOK), 0)
    expert = lax.broadcasted_iota(jnp.int32, (EXPERTS, TOK), 0)
    before = (
        lax.broadcasted_iota(jnp.int32, (TOK, TOK), 0)
        < lax.broadcasted_iota(jnp.int32, (TOK, TOK), 1)
    ).astype(jnp.bfloat16)

    def choose(r, g, s):
        named0 = (expert == r[0:1]).astype(jnp.float32)
        named1 = (expert == r[1:2]).astype(jnp.float32)
        earlier = jnp.dot(
            (named0 + named1).astype(jnp.bfloat16), before, preferred_element_type=jnp.float32
        )
        slot0 = jnp.sum(named0 * earlier, axis=0, keepdims=True).astype(jnp.int32)
        slot1 = jnp.sum(named1 * earlier, axis=0, keepdims=True).astype(jnp.int32)
        hit0 = row == r[0:1] * PAIR + s * CAP + slot0
        hit1 = row == r[1:2] * PAIR + s * CAP + slot1
        pick = jnp.where(hit0 | hit1, 1.0, 0.0).astype(jnp.bfloat16)
        weight = jnp.where(hit0, g[0:1], 0.0) + jnp.where(hit1, g[1:2], 0.0)
        return pick, jnp.sum(weight, axis=1, keepdims=True)

    mine = jnp.where(c == 0, tok[...], grad[...])
    pick, scale = choose(routes[...], gates[...], c)
    sel[c] = pick
    total = jnp.dot(pick, mine, preferred_element_type=jnp.float32)

    pl.semaphore_wait(barrier, len(others))

    def announce(r):
        pl.semaphore_signal(ready.at[r, 0], inc=1, device_id=up, device_id_type=MESH)
        pl.semaphore_signal(ready.at[r, 1], inc=1, device_id=down, device_id_type=MESH)

    def hear(r):
        pl.semaphore_wait(ready.at[r, 0], 1)
        pl.semaphore_wait(ready.at[r, 1], 1)

    announce(0)
    first = net.send(routes, route_buf, mate)
    second = net.send(gates, gate_buf, mate)
    third = net.make(tok, values, mate)

    @pl.when(c == 0)
    def _():
        pltpu.make_async_remote_copy(
            src_ref=grad, dst_ref=values, send_sem=send_sem.at[2], recv_sem=recv_sem.at[2],
            device_id=mate, device_id_type=MESH,
        ).start()

    @pl.when(c == 1)
    def _():
        third.start()

    first.wait_recv()
    second.wait_recv()
    hear(0)
    announce(1)
    pick, more = choose(route_buf[...], gate_buf[...], 1 - c)
    sel[1 - c] = pick
    scale = scale + more
    hear(1)
    announce(2)
    third.wait_recv()
    total = total + jnp.dot(pick, values[...], preferred_element_type=jnp.float32)
    total = total * jnp.where(c == 0, 1.0, scale)
    send_slots[...] = total.astype(jnp.bfloat16).reshape(EXPERTS, PAIR, QUARTER)

    def cols(q):
        return pl.ds(pl.multiple_of(q * QUARTER, QUARTER), QUARTER)

    ev = {}
    own_block = xy.at[c, k * 2 + y // 2, :, cols(x)]
    own_slots = send_slots.at[z * 2 + y // 2]
    ev["r", 0, "a"] = net.send(own_slots, own_block, to_right)
    ev["l", 0, "a"] = net.send(own_slots, own_block, to_left)
    ev["y", 0, "a"] = net.send(own_slots, own_block, to_y)
    heard = 2
    for n, dz in enumerate(NEAR):
        while heard < min(dz, Z - dz):
            hear(heard)
            heard += 1
            if heard < 4:
                announce(heard)
        ze = (z + dz) % Z
        for j in range(2):
            src = send_slots.at[ze * 2 + (y // 2 if j == 0 else 1 - y // 2)]
            dst = xy.at[c, n * 4 + k * 2 + y // 2, :, cols(x)]
            if dz == 0 and j == 0:
                local_slots = pltpu.make_async_copy(src, dst, own_sem.at[2])
                local_slots.start()
            else:
                ev["z", n, j] = net.send(src, dst, device(ze, y if j == 0 else 3 - y, c, x))

    def share(key, block, count, q, target):
        ref = xy.at[c, pl.ds(block, count), :, cols(q)]
        ev[key] = net.send(ref, ref, target)

    def got(*keys):
        for name in keys:
            for key in (name, name + ("a",)):
                if key in ev and key not in done:
                    done.add(key)
                    ev[key].wait_recv()

    done = set()

    def step_A(n):
        if n == 0:
            local_slots.wait()
        else:
            got(("z", n, 0))
        got(("z", n, 1))
        own, count = (k * 2 + 1 - y // 2, 1) if n == 0 else (n * 4 + k * 2, 2)
        share(("r", n), own, count, x, to_right)
        share(("l", n), own, count, x, to_left)
        share(("y", n), own, count, x, to_y)

    def step_B(n):
        got(("y", n))
        other = n * 4 + (1 - k) * 2
        share(("r2", n), other, 2, x, to_right)
        share(("l2", n), other, 2, x, to_left)

    def step_Cr(n):
        got(("r", n), ("r2", n))
        share(("fr", n), n * 4, 2, left, to_right)

    def step_Cl(n):
        got(("l", n), ("l2", n))
        share(("fl", n), n * 4 + 2, 2, right, to_left)

    def step_Br(n):
        got(("r", n))
        own = n * 4 + k * 2
        share(("fr", n), own, 1, left, to_right)
        share(("y1", n), own, 2, left, to_y)

    def step_Bl(n):
        got(("l", n))
        own = n * 4 + k * 2
        share(("fl", n), own + 1, 1, right, to_left)
        share(("y2", n), own, 2, right, to_y)

    def step_C(n):
        got(("fr", n), ("fl", n))
        share(("y3", n), n * 4 + k * 2, 2, far, to_y)
        ref = xy.at[c, pl.ds(n * 4 + k * 2, 2)]
        ev["m", n, "a"] = net.send(ref, ref, mate)

    def step_D(n):
        if MODES[n]:
            got(("y", n), ("y1", n), ("y2", n), ("y3", n))
            ref = xy.at[c, pl.ds(n * 4 + (1 - k) * 2, 2)]
        else:
            got(("fr", n), ("fl", n))
            ref = xy.at[c, pl.ds(n * 4, 4)]
        ev["m", n] = net.send(ref, ref, mate)

    def step_F(g):
        if g == 0:
            up_copy.wait()
            down_copy.wait()
        got(*[("m", n) for n in GROUPS[g]])
        first_block, count = GROUPS[g][0] * 4, len(GROUPS[g]) * 4
        rows, size = pl.ds(first_block * PAIR, count * PAIR), count * PAIR
        rows_x = xy[0, pl.ds(first_block, count)].reshape(size, D)
        rows_y = xy[1, pl.ds(first_block, count)].reshape(size, D)
        pre = jnp.dot(rows_x, wu[...], preferred_element_type=jnp.float32)
        d_act = lax.dot_general(
            rows_y, wd[...], (((1,), (1,)), ((), ())), preferred_element_type=jnp.float32
        )
        act[rows] = gelu_value(pre).astype(jnp.bfloat16)
        slope = (d_act * gelu_slope(pre)).astype(jnp.bfloat16)
        d_pre[rows] = slope
        product = lax.dot_general(
            slope, wu[...], (((1,), (1,)), ((), ())), preferred_element_type=jnp.float32
        )
        for q in range(4):
            for h in range(2):
                at = q * QUARTER + h * HALF
                part[h, q, pl.ds(first_block, count)] = (
                    product[:, at : at + HALF].astype(jnp.bfloat16).reshape(count, PAIR, HALF)
                )
        for n in GROUPS[g]:
            ev["p", n] = net.send(
                part.at[1 - c, :, pl.ds(n * 4, 4)], from_mate.at[:, pl.ds(n * 4, 4)], mate
            )

    def wide(value):
        return value.astype(jnp.float32)

    def add(ref, other):
        ref[...] = (wide(ref[...]) + wide(other[...])).astype(jnp.bfloat16)

    def step_RA(n):
        got(("p", n))
        for q in range(4):
            acc[q, pl.ds(n * 4, 4)] = (
                wide(part[c, q, pl.ds(n * 4, 4)]) + wide(from_mate[q, pl.ds(n * 4, 4)])
            ).astype(jnp.bfloat16)
        if RETURN_MODES[n] == 2:
            ev["br", n] = net.send(acc.at[right, pl.ds(n * 4, 4)], hop_b.at[n, 0], to_right)
            ev["bl", n] = net.send(acc.at[left, pl.ds(n * 4, 4)], hop_b.at[n, 1], to_left)
            ev["far", n] = net.send(acc.at[far, pl.ds(n * 4, 4)], hop_c.at[n], to_far)
        elif RETURN_MODES[n] == 1:
            ev["ry", n] = net.send(
                acc.at[pl.ds(0, 4), pl.ds(n * 4 + (1 - k) * 2, 2)], from_y.at[n], to_y
            )
        else:
            ev["ar", n] = net.send(acc.at[far, pl.ds(n * 4, 2)], hop_a.at[n, 0], to_right)
            ev["al", n] = net.send(acc.at[far, pl.ds(n * 4 + 2, 2)], hop_a.at[n, 1], to_left)

    def step_RY(n):
        got(("ry", n))
        own = n * 4 + k * 2
        add(acc.at[pl.ds(0, 4), pl.ds(own, 2)], from_y.at[n])
        ev["ar", n] = net.send(acc.at[far, pl.ds(own, 1)], hop_a.at[n, 0, pl.ds(0, 1)], to_right)
        ev["al", n] = net.send(acc.at[far, pl.ds(own + 1, 1)], hop_a.at[n, 1, pl.ds(0, 1)], to_left)

    def step_RB(n):
        got(("ar", n))
        if RETURN_MODES[n]:
            own = n * 4 + k * 2
            add(acc.at[right, pl.ds(own, 1)], hop_a.at[n, 0, pl.ds(0, 1)])
            ev["br", n] = net.send(acc.at[right, pl.ds(own, 2)], hop_b.at[n, 0, pl.ds(0, 2)], to_right)
        else:
            add(acc.at[right, pl.ds(n * 4, 2)], hop_a.at[n, 0])
            ev["br", n] = net.send(acc.at[right, pl.ds(n * 4, 4)], hop_b.at[n, 0], to_right)

    def step_RX(n):
        got(("al", n))
        if RETURN_MODES[n]:
            own = n * 4 + k * 2
            add(acc.at[left, pl.ds(own + 1, 1)], hop_a.at[n, 1, pl.ds(0, 1)])
            ev["bl", n] = net.send(acc.at[left, pl.ds(own, 2)], hop_b.at[n, 1, pl.ds(0, 2)], to_left)
        else:
            add(acc.at[left, pl.ds(n * 4 + 2, 2)], hop_a.at[n, 1])
            ev["bl", n] = net.send(acc.at[left, pl.ds(n * 4, 4)], hop_b.at[n, 1], to_left)

    me = z * 2 + y // 2

    def step_RC(n):
        got(("br", n), ("bl", n))
        own = n * 4 + k * 2
        single = RETURN_MODES[n] == 1
        block, count = (own, 2) if single else (n * 4, 4)
        ref = acc.at[x, pl.ds(block, count)]
        total = (
            wide(ref[...]) + wide(hop_b[n, 0, pl.ds(0, count)]) + wide(hop_b[n, 1, pl.ds(0, count)])
        )
        if RETURN_MODES[n] == 2:
            got(("far", n))
            total = total + wide(hop_c[n])
        ref[...] = total.astype(jnp.bfloat16)
        zs = (z + Z - NEAR[n]) % Z
        other = n * 4 + (1 - k) * 2
        for j in range(2 if single else 4):
            row = y if j % 2 == 0 else 3 - y
            block = own if j < 2 else other
            block = block + (y // 2 if j % 2 == 0 else 1 - y // 2)
            if j >= 2:
                row = partner if j % 2 == 0 else 3 - partner
            dst = slots.at[j // 2, me]
            if n == 0 and j == 0:
                ev["own_back"] = pltpu.make_async_copy(acc.at[x, block], dst, own_sem.at[3])
                ev["own_back"].start()
            else:
                ev["back", n, j] = net.send(acc.at[x, block], dst, device(zs, row, c, x))

    def step_GU(i):
        tile = xy[0, :, :, i * TILE : (i + 1) * TILE].reshape(ROWS, TILE)
        grad_up[i * TILE : (i + 1) * TILE] = lax.dot_general(
            tile, d_pre[...], (((0,), (0,)), ((), ())), preferred_element_type=jnp.float32
        )

    def step_GD(i):
        tile = xy[1, :, :, i * TILE : (i + 1) * TILE].reshape(ROWS, TILE)
        grad_down[:, i * TILE : (i + 1) * TILE] = lax.dot_general(
            act[...], tile, (((0,), (0,)), ((), ())), preferred_element_type=jnp.float32
        )

    steps = dict(
        A=step_A, B=step_B, Br=step_Br, Bl=step_Bl, Cr=step_Cr, Cl=step_Cl, C=step_C, D=step_D,
        F=step_F, RA=step_RA, RY=step_RY, RB=step_RB, RX=step_RX, RC=step_RC,
        GU=step_GU, GD=step_GD,
    )
    for name in ORDER:
        steps[name[:-1]](int(name[-1]))

    for key in list(ev):
        if key[0] == "back":
            got(key)
    ev["own_back"].wait()
    def combine(s):
        total = jnp.zeros((TOK, HALF), jnp.float32)
        for h in range(2):
            total = total + lax.dot_general(
                sel[s],
                slots[h].reshape(EXPERTS * PAIR, HALF),
                (((0,), (0,)), ((), ())),
                preferred_element_type=jnp.float32,
            )
        return total.astype(jnp.bfloat16)

    result[0] = combine(1 - c)
    last = net.send(result.at[0], final, mate)
    result[1] = combine(c)
    last.wait_recv()

    @pl.when(c == 0)
    def _():
        out[:, 0:HALF] = result[1]
        out[:, HALF:QUARTER] = final[...]

    @pl.when(c == 1)
    def _():
        out[:, 0:HALF] = final[...]
        out[:, HALF:QUARTER] = result[1]

    net.finish()


def store_kernel(tok, up, down, tok_out, up_out, down_out, sem):
    copies = [pltpu.make_async_copy(tok, tok_out, sem.at[0])]
    for i in range(PARTS):
        for j, (src, dst) in enumerate(((up, up_out), (down, down_out))):
            size = src.shape[0] // PARTS
            rows = pl.ds(i * size, size)
            copies.append(pltpu.make_async_copy(src.at[rows], dst.at[rows], sem.at[1 + 2 * i + j]))
    for copy in copies:
        copy.start()
    for copy in copies:
        copy.wait()


def local(tokens, grad_out, routes, gates, w_up, w_down):
    bf16, f32 = jnp.bfloat16, jnp.float32
    inside = pl.BlockSpec(memory_space=pltpu.VMEM)
    anywhere = pl.BlockSpec(memory_space=pl.ANY)
    grads = pl.pallas_call(
        kernel,
        out_shape=(
            pltpu.VMEM((TOK, QUARTER), bf16),
            pltpu.VMEM((D, HID_DEV), f32),
            pltpu.VMEM((HID_DEV, D), f32),
        ),
        in_specs=[inside] * 4 + [anywhere] * 2,
        out_specs=(inside, inside, inside),
        scratch_shapes=[
            pltpu.VMEM((2, TOK), jnp.int32),
            pltpu.VMEM((2, TOK), f32),
            pltpu.VMEM((TOK, QUARTER), bf16),
            pltpu.VMEM((2, EXPERTS * PAIR, TOK), bf16),
            pltpu.VMEM((EXPERTS, PAIR, QUARTER), bf16),
            pltpu.VMEM((2, BLOCKS, PAIR, D), bf16),
            pltpu.VMEM((D, HID_DEV), bf16),
            pltpu.VMEM((HID_DEV, D), bf16),
            pltpu.VMEM((ROWS, HID_DEV), bf16),
            pltpu.VMEM((ROWS, HID_DEV), bf16),
            pltpu.VMEM((2, 4, BLOCKS, PAIR, HALF), bf16),
            pltpu.VMEM((4, BLOCKS, PAIR, HALF), bf16),
            pltpu.VMEM((4, BLOCKS, PAIR, HALF), bf16),
            pltpu.VMEM((Z, 2, 2, PAIR, HALF), bf16),
            pltpu.VMEM((Z, 2, 4, PAIR, HALF), bf16),
            pltpu.VMEM((Z, 4, PAIR, HALF), bf16),
            pltpu.VMEM((Z, 4, 2, PAIR, HALF), bf16),
            pltpu.VMEM((2, EXPERTS, PAIR, HALF), bf16),
            pltpu.VMEM((2, TOK, HALF), bf16),
            pltpu.VMEM((TOK, HALF), bf16),
            pltpu.SemaphoreType.DMA((224,)),
            pltpu.SemaphoreType.DMA((224,)),
            pltpu.SemaphoreType.DMA((4,)),
            pltpu.SemaphoreType.REGULAR((4, 2)),
        ],
        compiler_params=pltpu.CompilerParams(
            collective_id=0, has_side_effects=True, vmem_limit_bytes=VMEM_MIB * 1024 * 1024
        ),
        name="expert_backward",
    )(routes.T, gates.T, tokens, grad_out, w_up, w_down)
    return pl.pallas_call(
        store_kernel,
        out_shape=tuple(jax.ShapeDtypeStruct(g.shape, g.dtype) for g in grads),
        in_specs=[inside] * 3,
        out_specs=(anywhere,) * 3,
        scratch_shapes=[pltpu.SemaphoreType.DMA((1 + 2 * PARTS,))],
        compiler_params=pltpu.CompilerParams(vmem_limit_bytes=1024 * 1024),
        name="store_grads",
    )(*grads)


def solution(mesh):
    return jax.shard_map(
        local,
        mesh=mesh,
        in_specs=(
            P("expert", "tensor"),
            P("expert", "tensor"),
            P("expert", None),
            P("expert", None),
            P(None, ("expert", "tensor")),
            P(("expert", "tensor"), None),
        ),
        out_specs=(
            P("expert", "tensor"),
            P(None, ("expert", "tensor")),
            P(("expert", "tensor"), None),
        ),
        check_vma=False,
    )
```

```python
import jax
import jax.numpy as jnp
from jax import lax
from jax.experimental import pallas as pl
from jax.experimental.pallas import tpu as pltpu
from jax.sharding import PartitionSpec as P

MESH = pl.DeviceIdType.MESH
Z, Y, X = 8, 4, 4
CAP, PAIR = 20, 40
EXPERTS = 16
BLOCKS = 32
ROWS = BLOCKS * PAIR
TOK = 128
QUARTER = 512
HALF = 256
D = 2048
HID_DEV = 512
TILE = 256
PARTS = 1
VMEM_MIB = 48
NEAR = (0, 1, 7, 4, 3, 5, 2, 6)
MODES = (0, 1, 0, 1, 0, 0, 0, 1)
RETURN_MODES = (1, 0, 1, 2, 0, 0, 0, 1)
GROUPS = ((0, 1), (2, 3), (4, 5), (6, 7))
ORDER = (
    "A0", "A1", "A2", "B0", "Br1", "Bl1", "A3", "B2", "Cr0", "Cl0", "C1", "Br3", "Bl3", "A4", "A5",
    "Cr2", "Cl2", "D1", "A6", "A7", "D0", "C3", "F0", "B4", "D2", "B5", "RA0", "B6", "RA1", "Br7",
    "Bl7", "Cr4", "Cl4", "D3", "Cr5", "Cl5", "F1", "RY0", "Cr6", "Cl6", "RB1", "RX1", "C7", "D4",
    "RA2", "RA3", "D5", "D7", "RB0", "RX0", "D6", "F2", "RC1", "RY2", "F3", "RA4", "RA5", "GU0",
    "RC0", "RC3", "RB2", "RX2", "GD0", "RA6", "RA7", "GU1", "GD1", "RB4", "RX4", "GU2", "RB5",
    "RX5", "GD2", "RC2", "GU3", "RB6", "RX6", "GD3", "GU4", "RC4", "RY7", "RC5", "RB7", "RX7",
    "RC6", "RC7", "GD4", "GU5", "GD5", "GU6", "GD6", "GU7", "GD7",
)

root_half = 0.7071067811865476
gauss_norm = 0.3989422804014327


def gelu_value(v):
    return 0.5 * v * (1.0 + lax.erf(v * root_half))


def gelu_slope(v):
    return 0.5 * (1.0 + lax.erf(v * root_half)) + v * jnp.exp(-0.5 * v * v) * gauss_norm


def place():
    e = lax.axis_index("expert")
    x = lax.axis_index("tensor")
    return e // 8, (e // 2) % 4, e % 2, x


def device(z, y, c, x):
    return ((z * Y + y) * 2 + c, x)


class Net:
    def __init__(self, send_sem, recv_sem):
        self.send_sem, self.recv_sem, self.count, self.sent = send_sem, recv_sem, 0, []

    def make(self, src, dst, target):
        i = self.count
        self.count += 1
        copy = pltpu.make_async_remote_copy(
            src_ref=src,
            dst_ref=dst,
            send_sem=self.send_sem.at[i],
            recv_sem=self.recv_sem.at[i],
            device_id=target,
            device_id_type=MESH,
        )
        self.sent.append(copy)
        return copy

    def send(self, src, dst, target):
        copy = self.make(src, dst, target)
        copy.start()
        return copy

    def finish(self):
        for copy in self.sent:
            copy.wait_send()


def kernel(
    routes, gates, tok, grad, w_up, w_down,
    out, grad_up, grad_down,
    route_buf, gate_buf, values, sel, send_slots, xy, wu, wd, act, d_pre, part, from_mate, acc,
    hop_a, hop_b, hop_c, from_y, slots, result, final,
    send_sem, recv_sem, own_sem, ready,
):
    z, y, c, x = place()
    k = ((y + 1) // 2) % 2
    partner = y + 1 - 2 * (y % 2)
    net = Net(send_sem, recv_sem)
    mate = device(z, y, 1 - c, x)
    right, left, far = (x + 1) % X, (x + 3) % X, (x + 2) % X
    to_right, to_left = device(z, y, c, right), device(z, y, c, left)
    to_y, to_far = device(z, partner, c, x), device(z, y, c, far)

    slots[...] = jnp.zeros_like(slots)
    up, down = device((z + 1) % Z, y, c, x), device((z + Z - 1) % Z, y, c, x)
    others = [mate, to_right, to_left, to_y, device(z, 3 - y, c, x), up, down]
    barrier = pltpu.get_barrier_semaphore()
    for other in others:
        pl.semaphore_signal(barrier, inc=1, device_id=other, device_id_type=MESH)

    up_copy = pltpu.make_async_copy(w_up, wu, own_sem.at[0])
    down_copy = pltpu.make_async_copy(w_down, wd, own_sem.at[1])
    up_copy.start()
    down_copy.start()

    row = lax.broadcasted_iota(jnp.int32, (EXPERTS * PAIR, TOK), 0)
    expert = lax.broadcasted_iota(jnp.int32, (EXPERTS, TOK), 0)
    before = (
        lax.broadcasted_iota(jnp.int32, (TOK, TOK), 0)
        < lax.broadcasted_iota(jnp.int32, (TOK, TOK), 1)
    ).astype(jnp.bfloat16)

    def choose(r, g, s):
        named0 = (expert == r[0:1]).astype(jnp.float32)
        named1 = (expert == r[1:2]).astype(jnp.float32)
        earlier = jnp.dot(
            (named0 + named1).astype(jnp.bfloat16), before, preferred_element_type=jnp.float32
        )
        slot0 = jnp.sum(named0 * earlier, axis=0, keepdims=True).astype(jnp.int32)
        slot1 = jnp.sum(named1 * earlier, axis=0, keepdims=True).astype(jnp.int32)
        hit0 = row == r[0:1] * PAIR + s * CAP + slot0
        hit1 = row == r[1:2] * PAIR + s * CAP + slot1
        pick = jnp.where(hit0 | hit1, 1.0, 0.0).astype(jnp.bfloat16)
        weight = jnp.where(hit0, g[0:1], 0.0) + jnp.where(hit1, g[1:2], 0.0)
        return pick, jnp.sum(weight, axis=1, keepdims=True)

    mine = jnp.where(c == 0, tok[...], grad[...])
    pick, scale = choose(routes[...], gates[...], c)
    sel[c] = pick
    total = jnp.dot(pick, mine, preferred_element_type=jnp.float32)

    pl.semaphore_wait(barrier, len(others))

    def announce(r):
        pl.semaphore_signal(ready.at[r, 0], inc=1, device_id=up, device_id_type=MESH)
        pl.semaphore_signal(ready.at[r, 1], inc=1, device_id=down, device_id_type=MESH)

    def hear(r):
        pl.semaphore_wait(ready.at[r, 0], 1)
        pl.semaphore_wait(ready.at[r, 1], 1)

    announce(0)
    first = net.send(routes, route_buf, mate)
    second = net.send(gates, gate_buf, mate)
    third = net.make(tok, values, mate)

    @pl.when(c == 0)
    def _():
        pltpu.make_async_remote_copy(
            src_ref=grad, dst_ref=values, send_sem=send_sem.at[2], recv_sem=recv_sem.at[2],
            device_id=mate, device_id_type=MESH,
        ).start()

    @pl.when(c == 1)
    def _():
        third.start()

    first.wait_recv()
    second.wait_recv()
    hear(0)
    announce(1)
    pick, more = choose(route_buf[...], gate_buf[...], 1 - c)
    sel[1 - c] = pick
    scale = scale + more
    hear(1)
    announce(2)
    third.wait_recv()
    total = total + jnp.dot(pick, values[...], preferred_element_type=jnp.float32)
    total = total * jnp.where(c == 0, 1.0, scale)
    send_slots[...] = total.astype(jnp.bfloat16).reshape(EXPERTS, PAIR, QUARTER)

    def cols(q):
        return pl.ds(pl.multiple_of(q * QUARTER, QUARTER), QUARTER)

    ev = {}
    own_block = xy.at[c, k * 2 + y // 2, :, cols(x)]
    own_slots = send_slots.at[z * 2 + y // 2]
    ev["r", 0, "a"] = net.send(own_slots, own_block, to_right)
    ev["l", 0, "a"] = net.send(own_slots, own_block, to_left)
    ev["y", 0, "a"] = net.send(own_slots, own_block, to_y)
    heard = 2
    for n, dz in enumerate(NEAR):
        while heard < min(dz, Z - dz):
            hear(heard)
            heard += 1
            if heard < 4:
                announce(heard)
        ze = (z + dz) % Z
        for j in range(2):
            src = send_slots.at[ze * 2 + (y // 2 if j == 0 else 1 - y // 2)]
            dst = xy.at[c, n * 4 + k * 2 + y // 2, :, cols(x)]
            if dz == 0 and j == 0:
                local_slots = pltpu.make_async_copy(src, dst, own_sem.at[2])
                local_slots.start()
            else:
                ev["z", n, j] = net.send(src, dst, device(ze, y if j == 0 else 3 - y, c, x))

    def share(key, block, count, q, target):
        ref = xy.at[c, pl.ds(block, count), :, cols(q)]
        ev[key] = net.send(ref, ref, target)

    def got(*keys):
        for name in keys:
            for key in (name, name + ("a",)):
                if key in ev and key not in done:
                    done.add(key)
                    ev[key].wait_recv()

    done = set()

    def step_A(n):
        if n == 0:
            local_slots.wait()
        else:
            got(("z", n, 0))
        got(("z", n, 1))
        own, count = (k * 2 + 1 - y // 2, 1) if n == 0 else (n * 4 + k * 2, 2)
        share(("r", n), own, count, x, to_right)
        share(("l", n), own, count, x, to_left)
        share(("y", n), own, count, x, to_y)

    def step_B(n):
        got(("y", n))
        other = n * 4 + (1 - k) * 2
        share(("r2", n), other, 2, x, to_right)
        share(("l2", n), other, 2, x, to_left)

    def step_Cr(n):
        got(("r", n), ("r2", n))
        share(("fr", n), n * 4, 2, left, to_right)

    def step_Cl(n):
        got(("l", n), ("l2", n))
        share(("fl", n), n * 4 + 2, 2, right, to_left)

    def step_Br(n):
        got(("r", n))
        own = n * 4 + k * 2
        share(("fr", n), own, 1, left, to_right)
        share(("y1", n), own, 2, left, to_y)

    def step_Bl(n):
        got(("l", n))
        own = n * 4 + k * 2
        share(("fl", n), own + 1, 1, right, to_left)
        share(("y2", n), own, 2, right, to_y)

    def step_C(n):
        got(("fr", n), ("fl", n))
        share(("y3", n), n * 4 + k * 2, 2, far, to_y)
        ref = xy.at[c, pl.ds(n * 4 + k * 2, 2)]
        ev["m", n, "a"] = net.send(ref, ref, mate)

    def step_D(n):
        if MODES[n]:
            got(("y", n), ("y1", n), ("y2", n), ("y3", n))
            ref = xy.at[c, pl.ds(n * 4 + (1 - k) * 2, 2)]
        else:
            got(("fr", n), ("fl", n))
            ref = xy.at[c, pl.ds(n * 4, 4)]
        ev["m", n] = net.send(ref, ref, mate)

    def step_F(g):
        if g == 0:
            up_copy.wait()
            down_copy.wait()
        got(*[("m", n) for n in GROUPS[g]])
        first_block, count = GROUPS[g][0] * 4, len(GROUPS[g]) * 4
        rows, size = pl.ds(first_block * PAIR, count * PAIR), count * PAIR
        rows_x = xy[0, pl.ds(first_block, count)].reshape(size, D)
        rows_y = xy[1, pl.ds(first_block, count)].reshape(size, D)
        pre = jnp.dot(rows_x, wu[...], preferred_element_type=jnp.float32)
        d_act = lax.dot_general(
            rows_y, wd[...], (((1,), (1,)), ((), ())), preferred_element_type=jnp.float32
        )
        act[rows] = gelu_value(pre).astype(jnp.bfloat16)
        slope = (d_act * gelu_slope(pre)).astype(jnp.bfloat16)
        d_pre[rows] = slope
        product = lax.dot_general(
            slope, wu[...], (((1,), (1,)), ((), ())), preferred_element_type=jnp.float32
        )
        for q in range(4):
            for h in range(2):
                at = q * QUARTER + h * HALF
                part[h, q, pl.ds(first_block, count)] = (
                    product[:, at : at + HALF].astype(jnp.bfloat16).reshape(count, PAIR, HALF)
                )
        for n in GROUPS[g]:
            ev["p", n] = net.send(
                part.at[1 - c, :, pl.ds(n * 4, 4)], from_mate.at[:, pl.ds(n * 4, 4)], mate
            )

    def wide(value):
        return value.astype(jnp.float32)

    def add(ref, other):
        ref[...] = (wide(ref[...]) + wide(other[...])).astype(jnp.bfloat16)

    def step_RA(n):
        got(("p", n))
        blocks = pl.ds(n * 4, 4)

        def both_cores(*quarters):
            for q in quarters:
                acc[q, blocks] = (wide(part[c, q, blocks]) + wide(from_mate[q, blocks])).astype(
                    jnp.bfloat16
                )

        if RETURN_MODES[n] == 2:
            both_cores(far, right, left)
            ev["br", n] = net.send(acc.at[right, pl.ds(n * 4, 4)], hop_b.at[n, 0], to_right)
            ev["bl", n] = net.send(acc.at[left, pl.ds(n * 4, 4)], hop_b.at[n, 1], to_left)
            ev["far", n] = net.send(acc.at[far, pl.ds(n * 4, 4)], hop_c.at[n], to_far)
            both_cores(x)
        elif RETURN_MODES[n] == 1:
            both_cores(0, 1, 2, 3)
            ev["ry", n] = net.send(
                acc.at[pl.ds(0, 4), pl.ds(n * 4 + (1 - k) * 2, 2)], from_y.at[n], to_y
            )
        else:
            both_cores(far)
            ev["ar", n] = net.send(acc.at[far, pl.ds(n * 4, 2)], hop_a.at[n, 0], to_right)
            ev["al", n] = net.send(acc.at[far, pl.ds(n * 4 + 2, 2)], hop_a.at[n, 1], to_left)
            both_cores(right, left, x)

    def step_RY(n):
        got(("ry", n))
        own = n * 4 + k * 2
        add(acc.at[pl.ds(0, 4), pl.ds(own, 2)], from_y.at[n])
        ev["ar", n] = net.send(acc.at[far, pl.ds(own, 1)], hop_a.at[n, 0, pl.ds(0, 1)], to_right)
        ev["al", n] = net.send(acc.at[far, pl.ds(own + 1, 1)], hop_a.at[n, 1, pl.ds(0, 1)], to_left)

    def step_RB(n):
        got(("ar", n))
        if RETURN_MODES[n]:
            own = n * 4 + k * 2
            add(acc.at[right, pl.ds(own, 1)], hop_a.at[n, 0, pl.ds(0, 1)])
            ev["br", n] = net.send(acc.at[right, pl.ds(own, 2)], hop_b.at[n, 0, pl.ds(0, 2)], to_right)
        else:
            add(acc.at[right, pl.ds(n * 4, 2)], hop_a.at[n, 0])
            ev["br", n] = net.send(acc.at[right, pl.ds(n * 4, 4)], hop_b.at[n, 0], to_right)

    def step_RX(n):
        got(("al", n))
        if RETURN_MODES[n]:
            own = n * 4 + k * 2
            add(acc.at[left, pl.ds(own + 1, 1)], hop_a.at[n, 1, pl.ds(0, 1)])
            ev["bl", n] = net.send(acc.at[left, pl.ds(own, 2)], hop_b.at[n, 1, pl.ds(0, 2)], to_left)
        else:
            add(acc.at[left, pl.ds(n * 4 + 2, 2)], hop_a.at[n, 1])
            ev["bl", n] = net.send(acc.at[left, pl.ds(n * 4, 4)], hop_b.at[n, 1], to_left)

    me = z * 2 + y // 2

    def step_RC(n):
        got(("br", n), ("bl", n))
        own = n * 4 + k * 2
        single = RETURN_MODES[n] == 1
        block, count = (own, 2) if single else (n * 4, 4)
        ref = acc.at[x, pl.ds(block, count)]
        total = (
            wide(ref[...]) + wide(hop_b[n, 0, pl.ds(0, count)]) + wide(hop_b[n, 1, pl.ds(0, count)])
        )
        if RETURN_MODES[n] == 2:
            got(("far", n))
            total = total + wide(hop_c[n])
        ref[...] = total.astype(jnp.bfloat16)
        zs = (z + Z - NEAR[n]) % Z
        other = n * 4 + (1 - k) * 2
        for j in range(2 if single else 4):
            row = y if j % 2 == 0 else 3 - y
            block = own if j < 2 else other
            block = block + (y // 2 if j % 2 == 0 else 1 - y // 2)
            if j >= 2:
                row = partner if j % 2 == 0 else 3 - partner
            dst = slots.at[j // 2, me]
            if n == 0 and j == 0:
                ev["own_back"] = pltpu.make_async_copy(acc.at[x, block], dst, own_sem.at[3])
                ev["own_back"].start()
            else:
                ev["back", n, j] = net.send(acc.at[x, block], dst, device(zs, row, c, x))

    def step_GU(i):
        tile = xy[0, :, :, i * TILE : (i + 1) * TILE].reshape(ROWS, TILE)
        grad_up[i * TILE : (i + 1) * TILE] = lax.dot_general(
            tile, d_pre[...], (((0,), (0,)), ((), ())), preferred_element_type=jnp.float32
        )

    def step_GD(i):
        tile = xy[1, :, :, i * TILE : (i + 1) * TILE].reshape(ROWS, TILE)
        grad_down[:, i * TILE : (i + 1) * TILE] = lax.dot_general(
            act[...], tile, (((0,), (0,)), ((), ())), preferred_element_type=jnp.float32
        )

    steps = dict(
        A=step_A, B=step_B, Br=step_Br, Bl=step_Bl, Cr=step_Cr, Cl=step_Cl, C=step_C, D=step_D,
        F=step_F, RA=step_RA, RY=step_RY, RB=step_RB, RX=step_RX, RC=step_RC,
        GU=step_GU, GD=step_GD,
    )
    for name in ORDER:
        steps[name[:-1]](int(name[-1]))

    for key in list(ev):
        if key[0] == "back":
            got(key)
    ev["own_back"].wait()
    def combine(s):
        total = jnp.zeros((TOK, HALF), jnp.float32)
        for h in range(2):
            total = total + lax.dot_general(
                sel[s],
                slots[h].reshape(EXPERTS * PAIR, HALF),
                (((0,), (0,)), ((), ())),
                preferred_element_type=jnp.float32,
            )
        return total.astype(jnp.bfloat16)

    result[0] = combine(1 - c)
    last = net.send(result.at[0], final, mate)
    result[1] = combine(c)
    last.wait_recv()

    @pl.when(c == 0)
    def _():
        out[:, 0:HALF] = result[1]
        out[:, HALF:QUARTER] = final[...]

    @pl.when(c == 1)
    def _():
        out[:, 0:HALF] = final[...]
        out[:, HALF:QUARTER] = result[1]

    net.finish()


def store_kernel(tok, up, down, tok_out, up_out, down_out, sem):
    copies = [pltpu.make_async_copy(tok, tok_out, sem.at[0])]
    for i in range(PARTS):
        for j, (src, dst) in enumerate(((up, up_out), (down, down_out))):
            size = src.shape[0] // PARTS
            rows = pl.ds(i * size, size)
            copies.append(pltpu.make_async_copy(src.at[rows], dst.at[rows], sem.at[1 + 2 * i + j]))
    for copy in copies:
        copy.start()
    for copy in copies:
        copy.wait()


def local(tokens, grad_out, routes, gates, w_up, w_down):
    bf16, f32 = jnp.bfloat16, jnp.float32
    inside = pl.BlockSpec(memory_space=pltpu.VMEM)
    anywhere = pl.BlockSpec(memory_space=pl.ANY)
    grads = pl.pallas_call(
        kernel,
        out_shape=(
            pltpu.VMEM((TOK, QUARTER), bf16),
            pltpu.VMEM((D, HID_DEV), f32),
            pltpu.VMEM((HID_DEV, D), f32),
        ),
        in_specs=[inside] * 4 + [anywhere] * 2,
        out_specs=(inside, inside, inside),
        scratch_shapes=[
            pltpu.VMEM((2, TOK), jnp.int32),
            pltpu.VMEM((2, TOK), f32),
            pltpu.VMEM((TOK, QUARTER), bf16),
            pltpu.VMEM((2, EXPERTS * PAIR, TOK), bf16),
            pltpu.VMEM((EXPERTS, PAIR, QUARTER), bf16),
            pltpu.VMEM((2, BLOCKS, PAIR, D), bf16),
            pltpu.VMEM((D, HID_DEV), bf16),
            pltpu.VMEM((HID_DEV, D), bf16),
            pltpu.VMEM((ROWS, HID_DEV), bf16),
            pltpu.VMEM((ROWS, HID_DEV), bf16),
            pltpu.VMEM((2, 4, BLOCKS, PAIR, HALF), bf16),
            pltpu.VMEM((4, BLOCKS, PAIR, HALF), bf16),
            pltpu.VMEM((4, BLOCKS, PAIR, HALF), bf16),
            pltpu.VMEM((Z, 2, 2, PAIR, HALF), bf16),
            pltpu.VMEM((Z, 2, 4, PAIR, HALF), bf16),
            pltpu.VMEM((Z, 4, PAIR, HALF), bf16),
            pltpu.VMEM((Z, 4, 2, PAIR, HALF), bf16),
            pltpu.VMEM((2, EXPERTS, PAIR, HALF), bf16),
            pltpu.VMEM((2, TOK, HALF), bf16),
            pltpu.VMEM((TOK, HALF), bf16),
            pltpu.SemaphoreType.DMA((224,)),
            pltpu.SemaphoreType.DMA((224,)),
            pltpu.SemaphoreType.DMA((4,)),
            pltpu.SemaphoreType.REGULAR((4, 2)),
        ],
        compiler_params=pltpu.CompilerParams(
            collective_id=0, has_side_effects=True, vmem_limit_bytes=VMEM_MIB * 1024 * 1024
        ),
        name="expert_backward",
    )(routes.T, gates.T, tokens, grad_out, w_up, w_down)
    return pl.pallas_call(
        store_kernel,
        out_shape=tuple(jax.ShapeDtypeStruct(g.shape, g.dtype) for g in grads),
        in_specs=[inside] * 3,
        out_specs=(anywhere,) * 3,
        scratch_shapes=[pltpu.SemaphoreType.DMA((1 + 2 * PARTS,))],
        compiler_params=pltpu.CompilerParams(vmem_limit_bytes=1024 * 1024),
        name="store_grads",
    )(*grads)


def solution(mesh):
    return jax.shard_map(
        local,
        mesh=mesh,
        in_specs=(
            P("expert", "tensor"),
            P("expert", "tensor"),
            P("expert", None),
            P("expert", None),
            P(None, ("expert", "tensor")),
            P(("expert", "tensor"), None),
        ),
        out_specs=(
            P("expert", "tensor"),
            P(None, ("expert", "tensor")),
            P(("expert", "tensor"), None),
        ),
        check_vma=False,
    )
```
